128 devices in a mesh: tile: 16 (over y_lo, z, core), mem: 8 (over y_hi, x).
Axes of the slice: x: 4, y: 4 (y_hi: 2, y_lo: 2; y = y_hi * 2 + y_lo), z: 4, core: 2. Of those that a mesh axis runs over, the one named last changes fastest.
Arguments:
- anomalies: bfloat16 [64, 2, 32, 65536], P('mem', None, None, 'tile'), may hold values from -0.75 to 0.75
- alpha0: float32 [64, 32, 65536], P('mem', None, 'tile'), may hold values from -33 to 33
- chi0: float32 [32, 65536], P('mem', 'tile'), may hold values from -5 to 5
- sigma: float32 [32, 65536], P('mem', 'tile'), may hold values from 0.3 to 1.5
- innov: float32 [2, 32, 65536], P(None, None, 'tile'), may hold values from -6 to 6
- rinv: float32 [2, 32, 65536], P(None, None, 'tile'), may hold values from 0.25 to 4
- taper_cols: int32 [512, 6], P('tile'), may hold values from 0 to 511, as said below
- taper_coef: bfloat16 [512, 6, 128, 128], P('tile'), may hold values from -0.21875 to 0.21875
Outputs:
- alpha_next: float32 [64, 32, 65536], P('mem', None, 'tile')
- chi_next: float32 [32, 65536], P('mem', 'tile')
- grad_alpha: float32 [64, 32, 65536], P('mem', None, 'tile')
- grad_chi: float32 [32, 65536], P('mem', 'tile')
The draws below stay inside these ranges and needn't reach their ends.
Inputs may be any that keep to these rules, and one draw needn't show every extreme that they name: `taper_cols`: block row i lists block i itself and 5 other distinct blocks whose cyclic distance from i (modulo 512) is at most 4, in no set order; on every device the first of its block rows lists the block 4 before it and the last lists the block 4 after it.
All inputs are finite; a program needn't handle non-finite values.
Results may differ from the reference program's by a relative error of at most 0.0085.
Values may be sent and summed in bfloat16 or wider, within the bound.
No kernel may reach another device: no remote copies, remote signals or barrier semaphores. Data moves between devices by JAX's collectives and lax.ppermute only.
A program may use at most 128 MiB of HBM per device.

```python
import math
import jax
import jax.numpy as jnp
from jax import lax

LEV = 32
T_SLOTS = 2
BLK = 128
W = 4
K = 6
NB = 32
MEMBERS = 64
NBTOT = 512
NCOLS = 65536


def draw_taper_cols(key, part):
    first_key, second_key = jax.random.split(key)
    block_rows = jnp.arange(NBTOT, dtype=jnp.int32)
    local_index = block_rows % NB
    slot_ids = jnp.arange(2 * W, dtype=jnp.int32)
    offsets = jnp.where(slot_ids < W, slot_ids - W, slot_ids - W + 1)
    scores = jax.random.randint(first_key, (NBTOT, 2 * W), 0, 1048576) * (2 * W) + slot_ids[None]
    forced = (local_index[:, None] == 0) & (slot_ids[None] == 0) | (local_index[:, None] == NB - 1) & (slot_ids[None] == 2 * W - 1)
    scores = jnp.where(forced, -1, scores)
    picked = jnp.argsort(scores, axis=1)[:, :K - 1]
    chosen = offsets[picked]
    offsets_all = jnp.concatenate([jnp.zeros((NBTOT, 1), jnp.int32), chosen.astype(jnp.int32)], axis=1)
    slot_order = jnp.argsort(jax.random.randint(second_key, (NBTOT, K), 0, 1048576) * K + jnp.arange(K, dtype=jnp.int32)[None], axis=1)
    offsets_all = jnp.take_along_axis(offsets_all, slot_order, axis=1)
    return ((block_rows[:, None] + offsets_all) % NBTOT).astype(jnp.int32)


def draw_alpha0(key, part):
    first_key, second_key, third_key = jax.random.split(key, 3)
    shape = (MEMBERS, LEV, NCOLS)
    position = jnp.arange(NCOLS, dtype=jnp.float32) / NCOLS
    row_scale = jnp.exp(jax.random.uniform(second_key, (MEMBERS, LEV, 1)) * math.log(10.0)) / math.sqrt(10.0)
    column_scale = jnp.exp(jax.random.uniform(third_key, (NCOLS,)) * math.log(10.0)) / math.sqrt(10.0)
    base = jax.random.truncated_normal(first_key, -4.0, 4.0, shape)
    ramp = jnp.exp((position - 0.5) * math.log(3.0))
    return (0.25 * base * row_scale * column_scale * ramp).astype(jnp.float32)


def block_scale(own_key, extent, cuts, low, largest):
    level, own = 1.0, jax.random.fold_in(own_key, 6)
    for axis_at, parts in cuts:
        steps = jnp.exp(jax.random.uniform(jax.random.fold_in(own, axis_at), (parts,), jnp.float32, low / len(cuts), largest / len(cuts)))
        level = level * jnp.repeat(steps, extent[axis_at] // parts).reshape([-1 if axis == axis_at else 1 for axis in range(len(extent))])
    return level


def bell_draw(own_key, dims, width, bound, cuts=(), held_as=jnp.bfloat16):
    level = block_scale(own_key, dims, cuts, -0.22, 0.18) if cuts else 1.0
    drawn = jax.random.normal(own_key, dims, jnp.float32) * width * level
    return jnp.minimum(jnp.maximum(drawn, -bound), bound).astype(held_as)


def setup_inputs(seed: int = 0) -> dict:
    arg_keys = jax.random.split(jax.random.key(seed), 9)
    return {
        "anomalies": bell_draw(arg_keys[0], (MEMBERS, T_SLOTS, LEV, NCOLS), 0.125, 0.75, ((0, 8), (3, 16))),
        "alpha0": draw_alpha0(jax.random.fold_in(arg_keys[8], 71), 0),
        "chi0": bell_draw(arg_keys[2], (LEV, NCOLS), 1.0, 5.0, ((0, 8), (1, 16)), jnp.float32),
        "sigma": jnp.clip(jnp.exp(math.log(1.5) - 1.60943787 * jax.random.uniform(arg_keys[3], (LEV, NCOLS), jnp.float32) ** block_scale(arg_keys[3], (LEV, NCOLS), ((0, 8), (1, 16)), -0.2, 0.2)), 0.3, 1.5),
        "innov": bell_draw(arg_keys[4], (T_SLOTS, LEV, NCOLS), 1.0, 6.0, ((2, 16),), jnp.float32),
        "rinv": jnp.clip(jnp.exp(math.log(4.0) - 2.7725887 * jax.random.uniform(arg_keys[5], (T_SLOTS, LEV, NCOLS), jnp.float32) ** block_scale(arg_keys[5], (T_SLOTS, LEV, NCOLS), ((2, 16),), -0.2, 0.2)), 0.25, 4.0),
        "taper_cols": draw_taper_cols(jax.random.fold_in(arg_keys[8], 71), 0),
        "taper_coef": bell_draw(arg_keys[7], (NBTOT, K, BLK, BLK), (K * BLK) ** -0.5, 0.21875, ((0, 16),)),
    }


def forward_member(rounded, taper_cols, coef_wide):
    picked = rounded[:, taper_cols].astype(jnp.float32)
    return jnp.einsum('ijpq,lijq->lip', coef_wide, picked)

def gradient(alpha, chi, anomalies, sigma, innov, rinv, taper_cols, coef_wide):
    block_count = taper_cols.shape[0]
    block_size = coef_wide.shape[2]
    members, levels, columns = alpha.shape

    def add_member(increment, pair):
        alpha_member, anomaly_member = pair
        rounded = alpha_member.astype(jnp.bfloat16).reshape(levels, block_count, block_size)
        localized = forward_member(rounded, taper_cols, coef_wide).reshape(levels, columns)
        return (increment + anomaly_member.astype(jnp.float32) * localized[None], None)
    start_value = jnp.broadcast_to((sigma * chi)[None], innov.shape).astype(jnp.float32)
    increment, _ = lax.scan(add_member, start_value, (alpha, anomalies))
    residual = (rinv * (increment - innov)).astype(jnp.bfloat16)
    residual_wide = lax.optimization_barrier(residual).astype(jnp.float32)

    def member_grad(pair):
        alpha_member, anomaly_member = pair
        weighted = jnp.einsum('tlc,tlc->lc', anomaly_member.astype(jnp.float32), residual_wide).astype(jnp.bfloat16)
        weighted_wide = lax.optimization_barrier(weighted).astype(jnp.float32).reshape(levels, block_count, block_size)
        contrib = jnp.einsum('ijpq,lip->lijq', coef_wide, weighted_wide)
        adjoint = jnp.zeros((levels, block_count, block_size), jnp.float32).at[:, taper_cols].add(contrib)
        return alpha_member + adjoint.reshape(levels, columns)
    grad_alpha = lax.map(member_grad, (alpha, anomalies))
    grad_chi = chi + sigma * lax.optimization_barrier(jnp.sum(residual_wide, axis=0))
    return (grad_alpha, grad_chi)

def reference(anomalies, alpha0, chi0, sigma, innov, rinv, taper_cols, taper_coef):
    coef_wide = taper_coef.astype(jnp.float32)
    g_alpha, g_chi = gradient(alpha0, chi0, anomalies, sigma, innov, rinv, taper_cols, coef_wide)
    h_alpha, h_chi = gradient(alpha0 - g_alpha, chi0 - g_chi, anomalies, sigma, innov, rinv, taper_cols, coef_wide)
    change_alpha = g_alpha - h_alpha
    change_chi = g_chi - h_chi
    grad_norm = jnp.sum(g_alpha * g_alpha) + jnp.sum(g_chi * g_chi)
    grad_change = jnp.sum(g_alpha * change_alpha) + jnp.sum(g_chi * change_chi)
    step_length = grad_norm / grad_change
    return (alpha0 - step_length * g_alpha, chi0 - step_length * g_chi, g_alpha - step_length * change_alpha, g_chi - step_length * change_chi)
```

```python
import functools
import jax
import jax.numpy as jnp
from jax import lax
from jax.experimental import pallas as pl
from jax.experimental.pallas import tpu as pltpu
from jax.sharding import PartitionSpec as P

W = 4
B = 128
F32 = jnp.float32
BF16 = jnp.bfloat16


def shifted(array, axis, by):
    size = lax.axis_size(axis)
    return lax.ppermute(array, axis, [(i, (i + by) % size) for i in range(size)])


def masked(full, me, share):
    level = lax.broadcasted_iota(jnp.int32, full.shape, 0)
    mine = jnp.logical_and(level >= me * share, level < (me + 1) * share)
    return jnp.where(mine, full, 0.0)


def spread(own, me, levels):
    share = own.shape[0]
    return masked(jnp.concatenate([own] * (levels // share), axis=0), me, share)


def gathered(full, share):
    parts = [full[g * share : (g + 1) * share] for g in range(full.shape[0] // share)]
    return functools.reduce(jnp.add, parts)


def localize_rows(cols, xs, coef_ref, anom_ref, base, out_store, static):
    rows, slots = coef_ref.shape[:2]
    members, slot_count, levels = anom_ref.shape[:3]
    for r in range(rows):
        lhs = jnp.concatenate([xs[cols[base + r, s]] for s in range(slots)], axis=1)
        rhs = jnp.concatenate([coef_ref[r, s] for s in range(slots)], axis=1)
        loc = lax.dot_general(
            lhs, rhs, (((1,), (1,)), ((), ())), preferred_element_type=F32
        ).reshape(members, levels, B)
        for t in range(slot_count):
            a = anom_ref[:, t, :, r * B : (r + 1) * B].astype(F32)
            inc = jnp.sum(a * loc, axis=0) + static[:, r * B : (r + 1) * B]
            out_store(t, r, inc)


def forward_first(scal, cols, alpha_ref, low_ref, high_ref, coef_ref, anom_ref, chi_ref, sig_ref, out_ref, xs):
    d = pl.program_id(0)
    members, levels, columns = alpha_ref.shape
    n = columns // B

    @pl.when(d == 0)
    def _():
        for b in range(W):
            xs[b] = low_ref[:, :, b * B : (b + 1) * B].reshape(members * levels, B)
            xs[W + n + b] = high_ref[:, :, b * B : (b + 1) * B].reshape(members * levels, B)
        for b in range(n):
            xs[W + b] = alpha_ref[:, :, b * B : (b + 1) * B].astype(BF16).reshape(members * levels, B)

    static = spread(sig_ref[...] * chi_ref[...], scal[0], levels)

    def store(t, r, inc):
        out_ref[0, t, :, r * B : (r + 1) * B] = inc.astype(BF16)

    localize_rows(cols, xs, coef_ref, anom_ref, d * coef_ref.shape[0], store, static)


def forward_second(
    scal, cols, alpha_ref, acc_ref, prev_ref, next_ref, coef_ref, anom_ref, chi_ref, sig_ref, res_ref,
    out_ref, norm_ref, xs, tot,
):
    d = pl.program_id(0)
    rows = coef_ref.shape[0]
    members, _, levels = anom_ref.shape[:3]
    n = acc_ref.shape[0] - 2 * W

    @pl.when(d == 0)
    def _():
        for b in range(n + 2 * W):
            v = acc_ref[b]
            if b < 2 * W:
                v = v + prev_ref[b].astype(F32)
            if b >= n:
                v = v + next_ref[b - n].astype(F32)
            xs[b] = (-v).astype(BF16)
        tot[...] = jnp.zeros_like(tot)

    rsum = res_ref[0, 0].astype(F32) + res_ref[0, 1].astype(F32)
    sig = spread(sig_ref[...], scal[0], levels)
    chi = spread(chi_ref[...], scal[0], levels)
    sr = sig * rsum
    static = -(sig * sr)
    gc = chi + sr
    sq = jnp.zeros((levels, B), F32)
    for r in range(rows):
        sq = sq + gc[:, r * B : (r + 1) * B] * gc[:, r * B : (r + 1) * B]
    tot[...] += sq

    def own_square(r, extra):
        adj = acc_ref[W + d * rows + r]
        if extra is not None:
            adj = adj + extra.astype(F32)
        g = alpha_ref[:, :, r * B : (r + 1) * B] + adj.reshape(members, levels, B)
        tot[...] += jnp.sum(g * g, axis=0)

    last = pl.num_programs(0) - 1
    edge = W // rows

    @pl.when(d == 0)
    def _():
        for r in range(rows):
            own_square(r, prev_ref[W + r])

    @pl.when(d == last)
    def _():
        for r in range(rows):
            own_square(r, next_ref[r])

    @pl.when(jnp.logical_and(d > 0, d < last))
    def _():
        for r in range(rows):
            own_square(r, None)

    def store(t, r, inc):
        out_ref[0, t, :, r * B : (r + 1) * B] = inc.astype(BF16)

    localize_rows(cols, xs, coef_ref, anom_ref, d * rows, store, static)

    @pl.when(d == last)
    def _():
        norm_ref[...] = tot[...]


def residual_first(scal, y_ref, rinv_ref, innov_ref, out_ref, inc_ref):
    y = jnp.sum(y_ref[...].astype(F32), axis=0)
    inc_ref[...] = y
    r = (rinv_ref[...] * (y - innov_ref[...])).astype(BF16)
    for k in range(out_ref.shape[0]):
        out_ref[k] = r


def residual_second(scal, y_ref, rinv_ref, innov_ref, inc_ref, old_ref, norm_ref, out_ref, sum_ref):
    y = jnp.sum(y_ref[...].astype(F32), axis=0)
    r = (rinv_ref[...] * (y - innov_ref[...])).astype(BF16)
    for k in range(out_ref.shape[0]):
        out_ref[k] = r
    change = (old_ref[0].astype(F32) - r.astype(F32)) * (inc_ref[...] - y)
    change = jnp.sum(change.reshape(-1, 8, change.shape[-1]), axis=0)
    norm = norm_ref[...].reshape(-1, 8, B).sum(axis=0)
    total_n = jnp.sum(norm)
    total_p = jnp.sum(change)
    lane = lax.broadcasted_iota(jnp.int32, sum_ref.shape, 1)
    sum_ref[...] = jnp.where(lane == 0, total_n, jnp.where(lane == 1, total_p, 0.0))


def adjoint_kernel(cols, res_ref, anom_ref, coef_ref, acc_ref, low_ref, high_ref):
    d = pl.program_id(0)
    rows, slots = coef_ref.shape[:2]
    members, slot_count, levels = anom_ref.shape[:3]
    n = acc_ref.shape[0] - 2 * W

    @pl.when(d == 0)
    def _():
        for b in range(n + 2 * W):
            acc_ref[b] = jnp.zeros(acc_ref.shape[1:], F32)

    for r in range(rows):
        sl = slice(r * B, (r + 1) * B)
        w = functools.reduce(
            jnp.add,
            [
                anom_ref[:, t, :, sl].astype(F32) * res_ref[0, t, :, sl].astype(F32)[None]
                for t in range(slot_count)
            ],
        )
        w = w.astype(BF16).reshape(members * levels, B)
        rhs = jnp.concatenate([coef_ref[r, s] for s in range(slots)], axis=1)
        part = jnp.dot(w, rhs, preferred_element_type=F32)
        for s in range(slots):
            c = cols[d * rows + r, s]
            acc_ref[c] += part[:, s * B : (s + 1) * B]

    @pl.when(d == pl.num_programs(0) - 1)
    def _():
        for b in range(low_ref.shape[0]):
            low_ref[b] = acc_ref[b].astype(BF16)
            high_ref[b] = acc_ref[n + 2 * W - high_ref.shape[0] + b].astype(BF16)


def final_kernel(
    scal, sums_ref, alpha_ref, acc1_ref, acc2_ref, prev1_ref, next1_ref, prev2_ref, next2_ref,
    chi_ref, sig_ref, res1_ref, res2_ref, an_ref, cn_ref, ga_ref, gc_ref,
):
    d = pl.program_id(0)
    rows = acc1_ref.shape[0]
    members, levels = alpha_ref.shape[:2]
    share = chi_ref.shape[0]
    totals = jnp.sum(sums_ref[...], axis=0, keepdims=True)
    lane = lax.broadcasted_iota(jnp.int32, totals.shape, 1)
    norm = jnp.sum(jnp.where(lane == 0, totals, 0.0), axis=1, keepdims=True)
    prod = norm + jnp.sum(jnp.where(lane == 1, totals, 0.0), axis=1, keepdims=True)
    step = norm / prod

    def rows_out(extra1, extra2):
        for r in range(rows):
            sl = slice(r * B, (r + 1) * B)
            a1 = acc1_ref[r]
            a2 = acc2_ref[r]
            if extra1 is not None:
                a1 = a1 + extra1(r).astype(F32)
                a2 = a2 + extra2(r).astype(F32)
            a1 = a1.reshape(members, levels, B)
            a2 = a2.reshape(members, levels, B)
            a0 = alpha_ref[:, :, sl]
            g = a0 + a1
            q = g + (a1 - a2)
            an_ref[:, :, sl] = a0 - step[None] * g
            ga_ref[:, :, sl] = g - step[None] * q

    last = pl.num_programs(0) - 1

    @pl.when(d == 0)
    def _():
        rows_out(lambda r: prev1_ref[W + r], lambda r: prev2_ref[r])

    @pl.when(d == last)
    def _():
        rows_out(lambda r: next1_ref[r], lambda r: next2_ref[r])

    @pl.when(jnp.logical_and(d > 0, d < last))
    def _():
        rows_out(None, None)

    s1 = res1_ref[0, 0].astype(F32) + res1_ref[0, 1].astype(F32)
    s2 = res2_ref[0, 0].astype(F32) + res2_ref[0, 1].astype(F32)
    s1 = gathered(masked(s1, scal[0], share), share)
    s2 = gathered(masked(s2, scal[0], share), share)
    chi = chi_ref[...]
    sg = sig_ref[...]
    g = chi + sg * s1
    q = g + (sg * s1 - sg * s2)
    cn_ref[...] = chi - step * g
    gc_ref[...] = g - step * q


def body(anomalies, alpha0, chi0, sigma, innov, rinv, taper_cols, taper_coef):
    members, levels, columns = alpha0.shape
    slot_count = anomalies.shape[1]
    nblocks, slots = taper_cols.shape
    share = chi0.shape[0]
    groups = lax.axis_size("mem")
    tiles = lax.axis_size("tile")
    me = lax.axis_index("mem")
    scal = me.astype(jnp.int32).reshape(1)
    rows = nblocks // groups
    width = rows * B
    ml = members * levels
    padded = nblocks + 2 * W
    cols = (taper_cols - lax.axis_index("tile") * nblocks + W) % (nblocks * tiles)

    whole = pl.BlockSpec(memory_space=pltpu.VMEM)
    coef_spec = pl.BlockSpec((rows, slots, B, B), lambda d, *_: (d, 0, 0, 0))
    anom_spec = pl.BlockSpec((members, slot_count, levels, width), lambda d, *_: (0, 0, 0, d))
    chi_spec = pl.BlockSpec((share, width), lambda d, *_: (0, d))
    alpha_spec = pl.BlockSpec((members, levels, width), lambda d, *_: (0, 0, d))
    piece_spec = pl.BlockSpec((1, slot_count, levels, width), lambda d, *_: (d, 0, 0, 0))
    pieces = jax.ShapeDtypeStruct((groups, slot_count, levels, width), BF16)
    own_spec = pl.BlockSpec((slot_count, levels, width), lambda d, s: (0, 0, s[0]))
    params = pltpu.CompilerParams(dimension_semantics=("arbitrary",), vmem_limit_bytes=60 * 2**20)

    low = shifted(alpha0[:, :, columns - W * B :].astype(BF16), "tile", 1)
    high = shifted(alpha0[:, :, : W * B].astype(BF16), "tile", -1)

    part1 = pl.pallas_call(
        forward_first,
        grid_spec=pltpu.PrefetchScalarGridSpec(
            num_scalar_prefetch=2,
            grid=(groups,),
            in_specs=[whole, whole, whole, coef_spec, anom_spec, chi_spec, chi_spec],
            out_specs=piece_spec,
            scratch_shapes=[pltpu.VMEM((padded, ml, B), BF16)],
        ),
        out_shape=pieces,
        compiler_params=params,
        name="forward_first",
    )(scal, cols, alpha0, low, high, taper_coef, anomalies, chi0, sigma)

    got1 = lax.all_to_all(part1, "mem", 0, 0)
    r1b, inc1 = pl.pallas_call(
        residual_first,
        grid_spec=pltpu.PrefetchScalarGridSpec(
            num_scalar_prefetch=1,
            grid=(1,),
            in_specs=[whole, own_spec, own_spec],
            out_specs=[whole, whole],
        ),
        out_shape=[pieces, jax.ShapeDtypeStruct((slot_count, levels, width), F32)],
        compiler_params=params,
        name="residual_first",
    )(scal, got1, rinv, innov)
    res1 = lax.all_to_all(r1b, "mem", 0, 0)

    def adjoint(res, halo, low_from):
        return pl.pallas_call(
            adjoint_kernel,
            grid_spec=pltpu.PrefetchScalarGridSpec(
                num_scalar_prefetch=1,
                grid=(groups,),
                in_specs=[piece_spec, anom_spec, coef_spec],
                out_specs=[whole, whole, whole],
            ),
            out_shape=[
                jax.ShapeDtypeStruct((padded, ml, B), F32),
                jax.ShapeDtypeStruct((halo, ml, B), BF16),
                jax.ShapeDtypeStruct((halo, ml, B), BF16),
            ],
            compiler_params=params,
            name="adjoint",
        )(cols, res, anomalies, taper_coef)

    acc1, low1, high1 = adjoint(res1, 2 * W, 0)
    prev1 = shifted(high1, "tile", 1)
    next1 = shifted(low1, "tile", -1)

    part2, norm = pl.pallas_call(
        forward_second,
        grid_spec=pltpu.PrefetchScalarGridSpec(
            num_scalar_prefetch=2,
            grid=(groups,),
            in_specs=[
                alpha_spec, whole, whole, whole, coef_spec, anom_spec, chi_spec, chi_spec, piece_spec,
            ],
            out_specs=[piece_spec, whole],
            scratch_shapes=[pltpu.VMEM((padded, ml, B), BF16), pltpu.VMEM((levels, B), F32)],
        ),
        out_shape=[pieces, jax.ShapeDtypeStruct((levels, B), F32)],
        compiler_params=params,
        name="forward_second",
    )(scal, cols, alpha0, acc1, prev1, next1, taper_coef, anomalies, chi0, sigma, res1)

    got2 = lax.all_to_all(part2, "mem", 0, 0)
    r2b, sums = pl.pallas_call(
        residual_second,
        grid_spec=pltpu.PrefetchScalarGridSpec(
            num_scalar_prefetch=1,
            grid=(1,),
            in_specs=[whole, own_spec, own_spec, whole, pl.BlockSpec((1, slot_count, levels, width), lambda d, s: (0, 0, 0, 0)), whole],
            out_specs=[whole, whole],
        ),
        out_shape=[pieces, jax.ShapeDtypeStruct((groups * tiles, B), F32)],
        compiler_params=params,
        name="residual_second",
    )(scal, got2, rinv, innov, inc1, r1b, norm)
    res2 = lax.all_to_all(r2b, "mem", 0, 0)
    sums = lax.all_to_all(sums, ("tile", "mem"), 0, 0, tiled=True)

    acc2, low2, high2 = adjoint(res2, W, 0)
    prev2 = shifted(high2, "tile", 1)
    next2 = shifted(low2, "tile", -1)

    acc_spec = pl.BlockSpec((rows, ml, B), lambda d, *_: (d + W // rows, 0, 0))
    out = pl.pallas_call(
        final_kernel,
        grid_spec=pltpu.PrefetchScalarGridSpec(
            num_scalar_prefetch=1,
            grid=(groups,),
            in_specs=[
                whole, alpha_spec, acc_spec, acc_spec, whole, whole, whole, whole,
                chi_spec, chi_spec, piece_spec, piece_spec,
            ],
            out_specs=[alpha_spec, chi_spec, alpha_spec, chi_spec],
        ),
        out_shape=[
            jax.ShapeDtypeStruct(alpha0.shape, F32),
            jax.ShapeDtypeStruct(chi0.shape, F32),
            jax.ShapeDtypeStruct(alpha0.shape, F32),
            jax.ShapeDtypeStruct(chi0.shape, F32),
        ],
        compiler_params=params,
        name="final",
    )(scal, sums, alpha0, acc1, acc2, prev1, next1, prev2, next2, chi0, sigma, res1, res2)
    return tuple(out)


def solution(mesh):
    placed = (
        P("mem", None, None, "tile"),
        P("mem", None, "tile"),
        P("mem", "tile"),
        P("mem", "tile"),
        P(None, None, "tile"),
        P(None, None, "tile"),
        P("tile", None),
        P("tile", None, None, None),
    )
    return jax.shard_map(
        body,
        mesh=mesh,
        in_specs=placed,
        out_specs=(
            P("mem", None, "tile"),
            P("mem", "tile"),
            P("mem", None, "tile"),
            P("mem", "tile"),
        ),
        check_vma=False,
    )
```

```python
import functools
import jax
import jax.numpy as jnp
from jax import lax
from jax.experimental import pallas as pl
from jax.experimental.pallas import tpu as pltpu
from jax.sharding import PartitionSpec as P

W = 4
B = 128
STREAMS = 1
F32 = jnp.float32
BF16 = jnp.bfloat16
MIB = 2**20


def shifted(array, axis, by):
    size = lax.axis_size(axis)
    return lax.ppermute(array, axis, [(i, (i + by) % size) for i in range(size)])


def resident(array):
    return pltpu.with_memory_space_constraint(array, pltpu.VMEM)


def masked(full, me, share, first):
    level = first + lax.broadcasted_iota(jnp.int32, full.shape, 0)
    mine = jnp.logical_and(level >= me * share, level < (me + 1) * share)
    return jnp.where(mine, full, 0.0)


def spread(own, me, levels, first):
    share = own.shape[0]
    return masked(jnp.concatenate([own] * (levels // share), axis=0), me, share, first)


def gathered(full, share):
    parts = [full[g * share : (g + 1) * share] for g in range(full.shape[0] // share)]
    return functools.reduce(jnp.add, parts)


def lanes(start, size):
    return pl.ds(pl.multiple_of(start, B), size)


def localize(first, levels, cols, xs, coef_ref, anom_ref, out_ref, static_of):
    groups = out_ref.shape[0]
    nblocks, slots = coef_ref.shape[:2]
    members, slot_count = anom_ref.shape[:2]
    rows = nblocks // groups
    lv = slice(first, first + levels)

    def step(d, carry):
        static = static_of(d)
        for r in range(rows):
            i = d * rows + r
            sl = slice(r * B, (r + 1) * B)
            lhs = jnp.concatenate([xs[cols[i, s]] for s in range(slots)], axis=1)
            rhs = jnp.concatenate([coef_ref[i, s] for s in range(slots)], axis=1)
            loc = lax.dot_general(
                lhs, rhs, (((1,), (1,)), ((), ())), preferred_element_type=F32
            ).reshape(members, levels, B)
            for t in range(slot_count):
                a = anom_ref[:, t, lv, lanes(i * B, B)].astype(F32)
                inc = jnp.sum(a * loc, axis=0) + static[:, sl]
                out_ref[d, t, :, sl] = inc.astype(BF16)
        return carry

    lax.fori_loop(0, groups, step, 0)


def forward_first(
    first, levels, me_ref, cols, alpha_ref, low_ref, high_ref, coef_ref, anom_ref, chi_ref, sig_ref,
    out_ref, xs,
):
    members, _, columns = alpha_ref.shape
    n = columns // B
    width = columns // out_ref.shape[0]
    ml = members * levels
    lv = slice(first, first + levels)
    for b in range(W):
        xs[b] = low_ref[:, lv, b * B : (b + 1) * B].reshape(ml, B)
        xs[W + n + b] = high_ref[:, lv, b * B : (b + 1) * B].reshape(ml, B)

    def load(b, carry):
        xs[W + b] = alpha_ref[:, lv, lanes(b * B, B)].astype(BF16).reshape(ml, B)
        return carry

    lax.fori_loop(0, n, load, 0, unroll=4)

    def static_of(d):
        cut = lanes(d * width, width)
        return spread(sig_ref[:, cut] * chi_ref[:, cut], me_ref[0], levels, first)

    localize(first, levels, cols, xs, coef_ref, anom_ref, out_ref, static_of)


def forward_second(
    first, levels, me_ref, cols, alpha_ref, acc_ref, prev_ref, next_ref, coef_ref, anom_ref, chi_ref,
    sig_ref, res_ref, out_ref, norm_ref, xs,
):
    members, _, columns = alpha_ref.shape
    n = columns // B
    groups = out_ref.shape[0]
    width = columns // groups
    lv = slice(first, first + levels)
    norm_ref[...] = jnp.zeros_like(norm_ref)

    def block(b, adj):
        xs[b] = (-adj).astype(BF16)

    def own(b, adj):
        block(b, adj)
        g = alpha_ref[:, lv, lanes((b - W) * B, B)] + adj.reshape(members, levels, B)
        norm_ref[...] += jnp.sum(g * g, axis=0)

    for b in range(W):
        block(b, acc_ref[b] + prev_ref[b].astype(F32))
        own(W + b, acc_ref[W + b] + prev_ref[W + b].astype(F32))
        own(n + b, acc_ref[n + b] + next_ref[b].astype(F32))
        block(n + W + b, acc_ref[n + W + b] + next_ref[W + b].astype(F32))

    def inner(b, carry):
        own(b, acc_ref[b])
        return carry

    lax.fori_loop(2 * W, n, inner, 0, unroll=2)

    def static_of(d):
        cut = lanes(d * width, width)
        rsum = res_ref[d, 0].astype(F32) + res_ref[d, 1].astype(F32)
        sig = spread(sig_ref[:, cut], me_ref[0], levels, first)
        chi = spread(chi_ref[:, cut], me_ref[0], levels, first)
        sr = sig * rsum
        gc = chi + sr
        sq = gc * gc
        for r in range(width // B):
            norm_ref[...] += sq[:, r * B : (r + 1) * B]
        return -(sig * sr)

    localize(first, levels, cols, xs, coef_ref, anom_ref, out_ref, static_of)


def residual_first(first, levels, me_ref, y_ref, rinv_ref, innov_ref, out_ref, inc_ref):
    width = y_ref.shape[-1]
    lv = slice(first, first + levels)
    cut = lanes(me_ref[0] * width, width)
    y = jnp.sum(y_ref[...].astype(F32), axis=0)
    inc_ref[...] = y
    r = (rinv_ref[:, lv, cut] * (y - innov_ref[:, lv, cut])).astype(BF16)
    for k in range(out_ref.shape[0]):
        out_ref[k] = r


def residual_second(
    first, levels, me_ref, y_ref, rinv_ref, innov_ref, inc_ref, old_ref, norm_ref, out_ref, sum_ref
):
    width = y_ref.shape[-1]
    lv = slice(first, first + levels)
    cut = lanes(me_ref[0] * width, width)
    y = jnp.sum(y_ref[...].astype(F32), axis=0)
    r = (rinv_ref[:, lv, cut] * (y - innov_ref[:, lv, cut])).astype(BF16)
    for k in range(out_ref.shape[0]):
        out_ref[k] = r
    change = (old_ref[0].astype(F32) - r.astype(F32)) * (inc_ref[...] - y)
    change = jnp.sum(change.reshape(-1, 8, width), axis=0)
    norm = norm_ref[...].reshape(-1, 8, B).sum(axis=0)
    lane = lax.broadcasted_iota(jnp.int32, sum_ref.shape, 1)
    sum_ref[...] = jnp.where(lane == 0, jnp.sum(norm), jnp.where(lane == 1, jnp.sum(change), 0.0))


def adjoint_kernel(first, levels, cols, res_ref, anom_ref, coef_ref, acc_ref, low_ref, high_ref):
    groups = res_ref.shape[0]
    nblocks, slots = coef_ref.shape[:2]
    members, slot_count = anom_ref.shape[:2]
    rows = nblocks // groups
    padded = nblocks + 2 * W
    ml = members * levels
    lv = slice(first, first + levels)

    def clear(b, carry):
        acc_ref[b] = jnp.zeros(acc_ref.shape[1:], F32)
        return carry

    lax.fori_loop(0, padded, clear, 0)

    def step(d, carry):
        for r in range(rows):
            i = d * rows + r
            sl = slice(r * B, (r + 1) * B)
            w = functools.reduce(
                jnp.add,
                [
                    anom_ref[:, t, lv, lanes(i * B, B)].astype(F32)
                    * res_ref[d, t, :, sl].astype(F32)[None]
                    for t in range(slot_count)
                ],
            )
            w = w.astype(BF16).reshape(ml, B)
            rhs = jnp.concatenate([coef_ref[i, s] for s in range(slots)], axis=1)
            part = jnp.dot(w, rhs, preferred_element_type=F32)
            for s in range(slots):
                acc_ref[cols[i, s]] += part[:, s * B : (s + 1) * B]
        return carry

    lax.fori_loop(0, groups, step, 0)
    halo = low_ref.shape[0]
    for b in range(halo):
        low_ref[b] = acc_ref[b].astype(BF16)
        high_ref[b] = acc_ref[padded - halo + b].astype(BF16)


def final_kernel(
    me_ref, sums_ref, alpha_ref, chi_ref, sig_ref, acc1, acc2, prev1, next1, prev2, next2, res1, res2,
    an_ref, cn_ref, ga_ref, gc_ref,
):
    d = pl.program_id(0)
    members, total, width = an_ref.shape
    streams = len(acc1)
    levels = total // streams
    rows = width // B
    share = chi_ref.shape[0]
    cut = lanes(d * width, width)
    totals = sum(jnp.sum(s[...], axis=0, keepdims=True) for s in sums_ref)
    lane = lax.broadcasted_iota(jnp.int32, totals.shape, 1)
    norm = jnp.sum(jnp.where(lane == 0, totals, 0.0), axis=1, keepdims=True)
    prod = norm + jnp.sum(jnp.where(lane == 1, totals, 0.0), axis=1, keepdims=True)
    step = norm / prod

    def rows_out(extra1, extra2):
        for h in range(streams):
            lv = slice(h * levels, (h + 1) * levels)
            for r in range(rows):
                sl = slice(r * B, (r + 1) * B)
                a1 = acc1[h][W + d * rows + r]
                a2 = acc2[h][W + d * rows + r]
                if extra1 is not None:
                    a1 = a1 + extra1(h, r).astype(F32)
                    a2 = a2 + extra2(h, r).astype(F32)
                a1 = a1.reshape(members, levels, B)
                a2 = a2.reshape(members, levels, B)
                a0 = alpha_ref[:, lv, lanes((d * rows + r) * B, B)]
                g = a0 + a1
                q = g + (a1 - a2)
                an_ref[:, lv, sl] = a0 - step[None] * g
                ga_ref[:, lv, sl] = g - step[None] * q

    last = pl.num_programs(0) - 1

    @pl.when(d == 0)
    def _():
        rows_out(lambda h, r: prev1[h][W + r], lambda h, r: prev2[h][r])

    @pl.when(d == last)
    def _():
        rows_out(lambda h, r: next1[h][r], lambda h, r: next2[h][r])

    @pl.when(jnp.logical_and(d > 0, d < last))
    def _():
        rows_out(None, None)

    def own_sum(res):
        parts = []
        for h in range(streams):
            s = res[h][d, 0].astype(F32) + res[h][d, 1].astype(F32)
            parts.append(gathered(masked(s, me_ref[0], share, h * levels), share))
        return functools.reduce(jnp.add, parts)

    s1 = own_sum(res1)
    s2 = own_sum(res2)
    chi = chi_ref[:, cut]
    sg = sig_ref[:, cut]
    g = chi + sg * s1
    q = g + (sg * s1 - sg * s2)
    cn_ref[...] = chi - step * g
    gc_ref[...] = g - step * q


def body(anomalies, alpha0, chi0, sigma, innov, rinv, taper_cols, taper_coef):
    members, all_levels, columns = alpha0.shape
    slot_count = anomalies.shape[1]
    nblocks, slots = taper_cols.shape
    share = chi0.shape[0]
    groups = lax.axis_size("mem")
    tiles = lax.axis_size("tile")
    me = lax.axis_index("mem").astype(jnp.int32).reshape(1)
    width = columns // groups
    levels = all_levels // STREAMS
    ml = members * levels
    padded = nblocks + 2 * W
    cols = (taper_cols - lax.axis_index("tile") * nblocks + W) % (nblocks * tiles)

    vm = pl.BlockSpec(memory_space=pltpu.VMEM)
    sm = pl.BlockSpec(memory_space=pltpu.SMEM)

    def call(kernel, name, scalars, operands, outs, scratch=(), limit=8):
        return pl.pallas_call(
            kernel,
            in_specs=[sm] * len(scalars) + [vm] * len(operands),
            out_specs=[vm] * len(outs),
            out_shape=[pltpu.VMEM(o.shape, o.dtype) for o in outs],
            scratch_shapes=list(scratch),
            compiler_params=pltpu.CompilerParams(vmem_limit_bytes=limit * MIB),
            name=name,
        )(*scalars, *[resident(o) for o in operands])

    pieces = jax.ShapeDtypeStruct((groups, slot_count, levels, width), BF16)
    inc_out = jax.ShapeDtypeStruct((slot_count, levels, width), F32)
    xs = pltpu.VMEM((padded, ml, B), BF16)
    part = functools.partial

    low = shifted(alpha0[:, :, columns - W * B :].astype(BF16), "tile", 1)
    high = shifted(alpha0[:, :, : W * B].astype(BF16), "tile", -1)

    def exchanged(x):
        return lax.all_to_all(x, "mem", 0, 0)

    def adjoint(first, res, halo):
        edge = jax.ShapeDtypeStruct((halo, ml, B), BF16)
        acc, lo, hi = call(
            part(adjoint_kernel, first, levels), "adjoint", [cols], [res, anomalies, taper_coef],
            [jax.ShapeDtypeStruct((padded, ml, B), F32), edge, edge],
        )
        return acc, shifted(hi, "tile", 1), shifted(lo, "tile", -1)

    firsts = [h * levels for h in range(STREAMS)]
    part1 = [
        call(
            part(forward_first, f, levels), "forward_first", [me, cols],
            [alpha0, low, high, taper_coef, anomalies, chi0, sigma], [pieces], [xs],
        )[0]
        for f in firsts
    ]
    got1 = [exchanged(p) for p in part1]
    own1 = [
        call(
            part(residual_first, f, levels), "residual_first", [me], [got, rinv, innov], [pieces, inc_out]
        )
        for f, got in zip(firsts, got1)
    ]
    res1 = [exchanged(o[0]) for o in own1]
    adj1 = [adjoint(f, res, 2 * W) for f, res in zip(firsts, res1)]
    part2 = [
        call(
            part(forward_second, f, levels), "forward_second", [me, cols],
            [alpha0, *adj, taper_coef, anomalies, chi0, sigma, res],
            [pieces, jax.ShapeDtypeStruct((levels, B), F32)], [xs],
        )
        for f, adj, res in zip(firsts, adj1, res1)
    ]
    got2 = [exchanged(p[0]) for p in part2]
    own2 = [
        call(
            part(residual_second, f, levels), "residual_second", [me],
            [got, rinv, innov, own[1], own[0], p[1]],
            [pieces, jax.ShapeDtypeStruct((groups * tiles, B), F32)],
        )
        for f, got, own, p in zip(firsts, got2, own1, part2)
    ]
    res2 = [exchanged(o[0]) for o in own2]
    sums = [lax.all_to_all(o[1], ("tile", "mem"), 0, 0, tiled=True) for o in own2]
    adj2 = [adjoint(f, res, W) for f, res in zip(firsts, res2)]

    operands = [
        sums, alpha0, chi0, sigma,
        [a[0] for a in adj1], [a[0] for a in adj2],
        [a[1] for a in adj1], [a[2] for a in adj1],
        [a[1] for a in adj2], [a[2] for a in adj2],
        res1, res2,
    ]
    flat, tree = jax.tree.flatten(operands)
    count = len(flat)

    def final(me_ref, *refs):
        final_kernel(me_ref, *jax.tree.unflatten(tree, refs[:count]), *refs[count:])

    alpha_spec = pl.BlockSpec((members, all_levels, width), lambda d: (0, 0, d))
    chi_spec = pl.BlockSpec((share, width), lambda d: (0, d))
    out = pl.pallas_call(
        final,
        grid=(groups,),
        in_specs=[sm] + [vm] * count,
        out_specs=[alpha_spec, chi_spec, alpha_spec, chi_spec],
        out_shape=[
            jax.ShapeDtypeStruct(alpha0.shape, F32),
            jax.ShapeDtypeStruct(chi0.shape, F32),
            jax.ShapeDtypeStruct(alpha0.shape, F32),
            jax.ShapeDtypeStruct(chi0.shape, F32),
        ],
        compiler_params=pltpu.CompilerParams(
            dimension_semantics=("arbitrary",), vmem_limit_bytes=8 * MIB
        ),
        name="final",
    )(me, *[resident(o) for o in flat])
    return tuple(out)


def solution(mesh):
    placed = (
        P("mem", None, None, "tile"),
        P("mem", None, "tile"),
        P("mem", "tile"),
        P("mem", "tile"),
        P(None, None, "tile"),
        P(None, None, "tile"),
        P("tile", None),
        P("tile", None, None, None),
    )
    return jax.shard_map(
        body,
        mesh=mesh,
        in_specs=placed,
        out_specs=(
            P("mem", None, "tile"),
            P("mem", "tile"),
            P("mem", None, "tile"),
            P("mem", "tile"),
        ),
        check_vma=False,
    )
```

```python
import functools
import jax
import jax.numpy as jnp
from jax import lax
from jax.experimental import pallas as pl
from jax.experimental.pallas import tpu as pltpu
from jax.sharding import PartitionSpec as P

W = 4
B = 128
F32 = jnp.float32
BF16 = jnp.bfloat16
MIB = 2**20


def shifted(array, axis, by):
    size = lax.axis_size(axis)
    return lax.ppermute(array, axis, [(i, (i + by) % size) for i in range(size)])


def resident(array):
    return pltpu.with_memory_space_constraint(array, pltpu.VMEM)


def masked(full, me, share, first):
    level = first + lax.broadcasted_iota(jnp.int32, full.shape, 0)
    mine = jnp.logical_and(level >= me * share, level < (me + 1) * share)
    return jnp.where(mine, full, 0.0)


def spread(own, me, levels, first):
    share = own.shape[0]
    return masked(jnp.concatenate([own] * (levels // share), axis=0), me, share, first)


def gathered(full, share):
    parts = [full[g * share : (g + 1) * share] for g in range(full.shape[0] // share)]
    return functools.reduce(jnp.add, parts)


def lanes(start, size):
    return pl.ds(pl.multiple_of(start, B), size)


def localize_group(d, levels, first, cols, xs, coef_ref, anom_ref, out_ref, static):
    groups = out_ref.shape[0]
    nblocks, slots = coef_ref.shape[:2]
    members, slot_count = anom_ref.shape[:2]
    rows = nblocks // groups
    lv = slice(first, first + levels)
    for r in range(rows):
        i = d * rows + r
        sl = slice(r * B, (r + 1) * B)
        lhs = jnp.concatenate([xs[cols[i, s]] for s in range(slots)], axis=1)
        rhs = jnp.concatenate([coef_ref[i, s] for s in range(slots)], axis=1)
        loc = lax.dot_general(
            lhs, rhs, (((1,), (1,)), ((), ())), preferred_element_type=F32
        ).reshape(members, levels, B)
        for t in range(slot_count):
            a = anom_ref[:, t, lv, lanes(i * B, B)].astype(F32)
            inc = jnp.sum(a * loc, axis=0) + static[:, sl]
            out_ref[d, t, :, sl] = inc.astype(BF16)


def first_static(d, width, levels, me_ref, chi_ref, sig_ref):
    cut = lanes(d * width, width)
    return spread(sig_ref[:, cut] * chi_ref[:, cut], me_ref[0], levels, 0)


def second_static(d, width, levels, me_ref, chi_ref, sig_ref, res_ref, norm_ref):
    cut = lanes(d * width, width)
    rsum = res_ref[d, 0].astype(F32) + res_ref[d, 1].astype(F32)
    sig = spread(sig_ref[:, cut], me_ref[0], levels, 0)
    chi = spread(chi_ref[:, cut], me_ref[0], levels, 0)
    sr = sig * rsum
    gc = chi + sr
    sq = gc * gc
    for r in range(width // B):
        norm_ref[...] += sq[:, r * B : (r + 1) * B]
    return -(sig * sr)


def edge_kernel(alpha_hbm, low_ref, high_ref, buf, sem):
    columns = alpha_hbm.shape[-1]
    width = low_ref.shape[-1]
    copies = [
        pltpu.make_async_copy(alpha_hbm.at[:, :, pl.ds(start, width)], buf.at[k], sem.at[k])
        for k, start in enumerate((0, columns - width))
    ]
    for c in copies:
        c.start()
    for c, out in zip(copies, (low_ref, high_ref)):
        c.wait()
        out[...] = buf[0 if out is low_ref else 1].astype(BF16)


def first_inner(
    me_ref, cols, alpha_hbm, coef_hbm, anom_hbm, chi_ref, sig_ref,
    alpha_ref, coef_ref, anom_ref, xs, out_ref, sem,
):
    members, levels, columns = alpha_ref.shape
    groups = out_ref.shape[0]
    width = columns // groups
    rows = width // B
    ml = members * levels

    def copy(kind, d):
        if kind == 0:
            part = (slice(None), slice(None), pl.ds(d * width, width))
            return pltpu.make_async_copy(alpha_hbm.at[part], alpha_ref.at[part], sem.at[kind, d])
        if kind == 1:
            part = pl.ds(d * rows, rows)
            return pltpu.make_async_copy(coef_hbm.at[part], coef_ref.at[part], sem.at[kind, d])
        part = (slice(None), slice(None), slice(None), pl.ds(d * width, width))
        return pltpu.make_async_copy(anom_hbm.at[part], anom_ref.at[part], sem.at[kind, d])

    order = [(0, 0), (0, 1)]
    for d in range(1, groups - 1):
        order += [(0, d + 1), (1, d), (2, d)]
    tail = [(k, d) for d in (0, groups - 1) for k in (1, 2)]
    for kind, d in order + tail:
        copy(kind, d).start()

    def load(d):
        copy(0, d).wait()
        for r in range(rows):
            b = d * rows + r
            xs[W + b] = alpha_ref[:, :, b * B : (b + 1) * B].astype(BF16).reshape(ml, B)

    load(0)
    load(1)
    for d in range(1, groups - 1):
        load(d + 1)
        copy(1, d).wait()
        copy(2, d).wait()
        static = first_static(d, width, levels, me_ref, chi_ref, sig_ref)
        localize_group(d, levels, 0, cols, xs, coef_ref, anom_ref, out_ref, static)
    for kind, d in tail:
        copy(kind, d).wait()


def first_outer(
    me_ref, cols, low_ref, high_ref, coef_ref, anom_ref, chi_ref, sig_ref, xs_in, part_ref, xs, out_ref
):
    members, _, levels, columns = anom_ref.shape
    groups = out_ref.shape[0]
    width = columns // groups
    ml = members * levels
    n = columns // B
    for b in range(W):
        xs[b] = low_ref[:, :, b * B : (b + 1) * B].reshape(ml, B)
        xs[W + n + b] = high_ref[:, :, b * B : (b + 1) * B].reshape(ml, B)

    def step(k, carry):
        d = k * (groups - 1)
        static = first_static(d, width, levels, me_ref, chi_ref, sig_ref)
        localize_group(d, levels, 0, cols, xs, coef_ref, anom_ref, out_ref, static)
        return carry

    lax.fori_loop(0, 2, step, 0)


def adjoint_group(d, cols, res_ref, anom_ref, coef_ref, acc_ref):
    groups = res_ref.shape[0]
    nblocks, slots = coef_ref.shape[:2]
    members, slot_count, levels = anom_ref.shape[:3]
    rows = nblocks // groups
    for r in range(rows):
        i = d * rows + r
        sl = slice(r * B, (r + 1) * B)
        w = functools.reduce(
            jnp.add,
            [
                anom_ref[:, t, :, lanes(i * B, B)].astype(F32) * res_ref[d, t, :, sl].astype(F32)[None]
                for t in range(slot_count)
            ],
        )
        w = w.astype(BF16).reshape(members * levels, B)
        rhs = jnp.concatenate([coef_ref[i, s] for s in range(slots)], axis=1)
        part = jnp.dot(w, rhs, preferred_element_type=F32)
        for s in range(slots):
            acc_ref[cols[i, s]] += part[:, s * B : (s + 1) * B]


def adjoint_edges(outer, cols, res_ref, anom_ref, coef_ref, acc_ref, low_ref, high_ref):
    groups = res_ref.shape[0]
    padded = acc_ref.shape[0]

    def clear(b, carry):
        acc_ref[b] = jnp.zeros(acc_ref.shape[1:], F32)
        return carry

    lax.fori_loop(0, padded, clear, 0)

    def step(k, carry):
        d = jnp.where(k < outer, k, groups - 2 * outer + k)
        adjoint_group(d, cols, res_ref, anom_ref, coef_ref, acc_ref)
        return carry

    lax.fori_loop(0, 2 * outer, step, 0)
    halo = low_ref.shape[0]
    for b in range(halo):
        low_ref[b] = acc_ref[b].astype(BF16)
        high_ref[b] = acc_ref[padded - halo + b].astype(BF16)


def adjoint_all(cols, res_ref, anom_ref, coef_ref, sum_in, acc_ref, low_ref, high_ref, sum_ref):
    adjoint_edges(res_ref.shape[0] // 2, cols, res_ref, anom_ref, coef_ref, acc_ref, low_ref, high_ref)


def adjoint_rest(outer, cols, res_ref, anom_ref, coef_ref, acc_in, acc_ref):
    def step(d, carry):
        adjoint_group(d, cols, res_ref, anom_ref, coef_ref, acc_ref)
        return carry

    lax.fori_loop(outer, res_ref.shape[0] - outer, step, 0)


def second_block(b, adj, alpha_ref, xs, norm_ref, own):
    members, levels = alpha_ref.shape[:2]
    xs[b] = (-adj).astype(BF16)
    if own:
        g = alpha_ref[:, :, lanes((b - W) * B, B)] + adj.reshape(members, levels, B)
        norm_ref[...] += jnp.sum(g * g, axis=0)


def second_inner(
    outer, me_ref, cols, res_ref, anom_ref, coef_ref, alpha_ref, chi_ref, sig_ref, acc_in,
    acc_ref, xs, out_ref, norm_ref,
):
    adjoint_rest(outer, cols, res_ref, anom_ref, coef_ref, acc_in, acc_ref)
    levels = alpha_ref.shape[1]
    groups = out_ref.shape[0]
    padded = acc_ref.shape[0]
    width = out_ref.shape[-1]
    norm_ref[...] = jnp.zeros_like(norm_ref)

    def block(b, carry):
        second_block(b, acc_ref[b], alpha_ref, xs, norm_ref, True)
        return carry

    lax.fori_loop(2 * W, padded - 2 * W, block, 0, unroll=2)

    def step(d, carry):
        static = second_static(d, width, levels, me_ref, chi_ref, sig_ref, res_ref, norm_ref)
        localize_group(d, levels, 0, cols, xs, coef_ref, anom_ref, out_ref, static)
        return carry

    lax.fori_loop(outer, groups - outer, step, 0)


def second_outer(
    outer, me_ref, cols, res_ref, anom_ref, coef_ref, alpha_ref, chi_ref, sig_ref, acc_ref, prev_ref,
    next_ref, xs_in, part_in, norm_in, xs, out_ref, norm_ref,
):
    levels = alpha_ref.shape[1]
    groups = out_ref.shape[0]
    width = out_ref.shape[-1]
    n = acc_ref.shape[0] - 2 * W
    for b in range(2 * W):
        second_block(b, acc_ref[b] + prev_ref[b].astype(F32), alpha_ref, xs, norm_ref, b >= W)
        second_block(n + b, acc_ref[n + b] + next_ref[b].astype(F32), alpha_ref, xs, norm_ref, b < W)

    def step(k, carry):
        d = jnp.where(k < outer, k, groups - 2 * outer + k)
        static = second_static(d, width, levels, me_ref, chi_ref, sig_ref, res_ref, norm_ref)
        localize_group(d, levels, 0, cols, xs, coef_ref, anom_ref, out_ref, static)
        return carry

    lax.fori_loop(0, 2 * outer, step, 0)


def residual_first(me_ref, y_ref, rinv_ref, innov_ref, out_ref, inc_ref):
    width = y_ref.shape[-1]
    cut = lanes(me_ref[0] * width, width)
    y = jnp.sum(y_ref[...].astype(F32), axis=0)
    inc_ref[...] = y
    r = (rinv_ref[:, :, cut] * (y - innov_ref[:, :, cut])).astype(BF16)
    for k in range(out_ref.shape[0]):
        out_ref[k] = r


def residual_second(
    me_ref, y_ref, rinv_ref, innov_ref, inc_ref, old_ref, norm_ref, out_ref, sum_ref
):
    width = y_ref.shape[-1]
    cut = lanes(me_ref[0] * width, width)
    y = jnp.sum(y_ref[...].astype(F32), axis=0)
    r = (rinv_ref[:, :, cut] * (y - innov_ref[:, :, cut])).astype(BF16)
    for k in range(out_ref.shape[0]):
        out_ref[k] = r
    change = (old_ref[0].astype(F32) - r.astype(F32)) * (inc_ref[...] - y)
    change = jnp.sum(change.reshape(-1, 8, width), axis=0)
    norm = norm_ref[...].reshape(-1, 8, B).sum(axis=0)
    lane = lax.broadcasted_iota(jnp.int32, sum_ref.shape, 1)
    sum_ref[...] = jnp.where(lane == 0, jnp.sum(norm), jnp.where(lane == 1, jnp.sum(change), 0.0))


def final_kernel(
    me_ref, sums_ref, alpha_ref, chi_ref, sig_ref, acc1, acc2, prev1, next1, prev2, next2, res1, res2,
    an_ref, cn_ref, ga_ref, gc_ref,
):
    d = pl.program_id(0)
    members, total, width = an_ref.shape
    streams = len(acc1)
    levels = total // streams
    rows = width // B
    share = chi_ref.shape[0]
    cut = lanes(d * width, width)
    totals = sum(jnp.sum(s[...], axis=0, keepdims=True) for s in sums_ref)
    lane = lax.broadcasted_iota(jnp.int32, totals.shape, 1)
    norm = jnp.sum(jnp.where(lane == 0, totals, 0.0), axis=1, keepdims=True)
    prod = norm + jnp.sum(jnp.where(lane == 1, totals, 0.0), axis=1, keepdims=True)
    step = norm / prod

    def rows_out(extra1, extra2):
        for h in range(streams):
            lv = slice(h * levels, (h + 1) * levels)
            for r in range(rows):
                sl = slice(r * B, (r + 1) * B)
                a1 = acc1[h][W + d * rows + r]
                a2 = acc2[h][W + d * rows + r]
                if extra1 is not None:
                    a1 = a1 + extra1(h, r).astype(F32)
                    a2 = a2 + extra2(h, r).astype(F32)
                a1 = a1.reshape(members, levels, B)
                a2 = a2.reshape(members, levels, B)
                a0 = alpha_ref[:, lv, lanes((d * rows + r) * B, B)]
                g = a0 + a1
                q = g + (a1 - a2)
                an_ref[:, lv, sl] = a0 - step[None] * g
                ga_ref[:, lv, sl] = g - step[None] * q

    last = pl.num_programs(0) - 1

    @pl.when(d == 0)
    def _():
        rows_out(lambda h, r: prev1[h][W + r], lambda h, r: prev2[h][r])

    @pl.when(d == last)
    def _():
        rows_out(lambda h, r: next1[h][r], lambda h, r: next2[h][r])

    @pl.when(jnp.logical_and(d > 0, d < last))
    def _():
        rows_out(None, None)

    def own_sum(res):
        parts = []
        for h in range(streams):
            s = res[h][d, 0].astype(F32) + res[h][d, 1].astype(F32)
            parts.append(gathered(masked(s, me_ref[0], share, h * levels), share))
        return functools.reduce(jnp.add, parts)

    s1 = own_sum(res1)
    s2 = own_sum(res2)
    chi = chi_ref[:, cut]
    sg = sig_ref[:, cut]
    g = chi + sg * s1
    q = g + (sg * s1 - sg * s2)
    cn_ref[...] = chi - step * g
    gc_ref[...] = g - step * q


def body(anomalies, alpha0, chi0, sigma, innov, rinv, taper_cols, taper_coef):
    members, all_levels, columns = alpha0.shape
    slot_count = anomalies.shape[1]
    nblocks, slots = taper_cols.shape
    share = chi0.shape[0]
    groups = lax.axis_size("mem")
    tiles = lax.axis_size("tile")
    me = lax.axis_index("mem").astype(jnp.int32).reshape(1)
    width = columns // groups
    levels = all_levels
    ml = members * levels
    padded = nblocks + 2 * W
    cols = (taper_cols - lax.axis_index("tile") * nblocks + W) % (nblocks * tiles)

    vm = pl.BlockSpec(memory_space=pltpu.VMEM)
    sm = pl.BlockSpec(memory_space=pltpu.SMEM)

    anywhere = pl.BlockSpec(memory_space=pltpu.HBM)
    part = functools.partial
    sds = jax.ShapeDtypeStruct
    pieces = sds((groups, slot_count, levels, width), BF16)
    inc_out = sds((slot_count, levels, width), F32)
    norm_out = sds((levels, B), F32)
    xs_out = sds((padded, ml, B), BF16)
    acc_out = sds((padded, ml, B), F32)
    work = 2 * ml * slots * B * B

    def call(kernel, name, scalars, operands, outs, scratch=(), limit=8, alias={}, hbm=0, rows=1):
        return pl.pallas_call(
            kernel,
            in_specs=[sm] * len(scalars) + [anywhere] * hbm + [vm] * (len(operands) - hbm),
            out_specs=[vm] * len(outs),
            out_shape=[pltpu.VMEM(o.shape, o.dtype) for o in outs],
            scratch_shapes=list(scratch),
            input_output_aliases={len(scalars) + k: v for k, v in alias.items()},
            compiler_params=pltpu.CompilerParams(vmem_limit_bytes=limit * MIB),
            cost_estimate=pl.CostEstimate(
                flops=8 * rows * work, transcendentals=0, bytes_accessed=rows * 3 * MIB // 4
            ),
            name=name,
        )(
            *scalars,
            *[pltpu.with_memory_space_constraint(o, pltpu.HBM) for o in operands[:hbm]],
            *[resident(o) for o in operands[hbm:]],
        )

    def exchanged(x):
        return lax.all_to_all(x, "mem", 0, 0)

    rim = sds((members, levels, W * B), BF16)
    high, low = call(
        edge_kernel, "edges", [], [alpha0], [rim, rim],
        [pltpu.VMEM((2, members, levels, W * B), F32), pltpu.SemaphoreType.DMA((2,))], hbm=1,
    )
    low = shifted(low, "tile", 1)
    high = shifted(high, "tile", -1)
    alpha, coef, anom, xs1, part1 = call(
        first_inner, "first_inner", [me, cols], [alpha0, taper_coef, anomalies, chi0, sigma],
        [sds(alpha0.shape, F32), sds(taper_coef.shape, BF16), sds(anomalies.shape, BF16), xs_out, pieces],
        [pltpu.SemaphoreType.DMA((3, groups))], hbm=3, rows=24,
    )
    xs1, part1 = call(
        first_outer, "first_outer", [me, cols], [low, high, coef, anom, chi0, sigma, xs1, part1],
        [xs_out, pieces], alias={6: 0, 7: 1}, rows=8,
    )
    got1 = exchanged(part1)
    r1, inc1 = call(residual_first, "residual_first", [me], [got1, rinv, innov], [pieces, inc_out])
    res1 = exchanged(r1)

    outer = 2 * W // (width // B)
    edge = sds((2 * W, ml, B), BF16)
    acc1, low1, high1 = call(
        part(adjoint_edges, outer), "adjoint_edges", [cols], [res1, anom, coef], [acc_out, edge, edge],
        rows=16,
    )
    prev1 = shifted(high1, "tile", 1)
    next1 = shifted(low1, "tile", -1)
    acc1, xs2, part2, norm = call(
        part(second_inner, outer), "second_inner", [me, cols],
        [res1, anom, coef, alpha, chi0, sigma, acc1], [acc_out, xs_out, pieces, norm_out],
        alias={6: 0}, rows=32,
    )
    xs2, part2, norm = call(
        part(second_outer, outer), "second_outer", [me, cols],
        [res1, anom, coef, alpha, chi0, sigma, acc1, prev1, next1, xs2, part2, norm],
        [xs_out, pieces, norm_out], alias={9: 0, 10: 1, 11: 2}, rows=16,
    )
    got2 = exchanged(part2)
    r2, sums = call(
        residual_second, "residual_second", [me], [got2, rinv, innov, inc1, r1, norm],
        [pieces, sds((groups * tiles, B), F32)],
    )
    res2 = exchanged(r2)
    edge = sds((W, ml, B), BF16)
    acc2, low2, high2, sums = call(
        adjoint_all, "adjoint_all", [cols], [res2, anom, coef, sums],
        [acc_out, edge, edge, sds(sums.shape, F32)], alias={3: 3}, rows=32,
    )
    prev2 = shifted(high2, "tile", 1)
    next2 = shifted(low2, "tile", -1)
    sums = lax.all_to_all(sums, ("tile", "mem"), 0, 0, tiled=True)
    operands = [
        [sums], alpha, chi0, sigma, [acc1], [acc2], [prev1], [next1], [prev2], [next2], [res1], [res2]
    ]
    flat, tree = jax.tree.flatten(operands)
    count = len(flat)

    def final(me_ref, *refs):
        final_kernel(me_ref, *jax.tree.unflatten(tree, refs[:count]), *refs[count:])

    alpha_spec = pl.BlockSpec((members, all_levels, width), lambda d: (0, 0, d))
    chi_spec = pl.BlockSpec((share, width), lambda d: (0, d))
    out = pl.pallas_call(
        final,
        grid=(groups,),
        in_specs=[sm] + [vm] * count,
        out_specs=[alpha_spec, chi_spec, alpha_spec, chi_spec],
        out_shape=[
            jax.ShapeDtypeStruct(alpha0.shape, F32),
            jax.ShapeDtypeStruct(chi0.shape, F32),
            jax.ShapeDtypeStruct(alpha0.shape, F32),
            jax.ShapeDtypeStruct(chi0.shape, F32),
        ],
        compiler_params=pltpu.CompilerParams(
            dimension_semantics=("arbitrary",), vmem_limit_bytes=8 * MIB
        ),
        name="final",
    )(me, *[resident(o) for o in flat])
    return tuple(out)


def solution(mesh):
    placed = (
        P("mem", None, None, "tile"),
        P("mem", None, "tile"),
        P("mem", "tile"),
        P("mem", "tile"),
        P(None, None, "tile"),
        P(None, None, "tile"),
        P("tile", None),
        P("tile", None, None, None),
    )
    return jax.shard_map(
        body,
        mesh=mesh,
        in_specs=placed,
        out_specs=(
            P("mem", None, "tile"),
            P("mem", "tile"),
            P("mem", None, "tile"),
            P("mem", "tile"),
        ),
        check_vma=False,
    )
```

```python
import functools
import jax
import jax.numpy as jnp
from jax import lax
from jax.experimental import pallas as pl
from jax.experimental.pallas import tpu as pltpu
from jax.sharding import PartitionSpec as P

W = 4
B = 128
F32 = jnp.float32
BF16 = jnp.bfloat16
MIB = 2**20


def shifted(array, axis, by):
    size = lax.axis_size(axis)
    return lax.ppermute(array, axis, [(i, (i + by) % size) for i in range(size)])


def resident(array):
    return pltpu.with_memory_space_constraint(array, pltpu.VMEM)


def column(cols, i, s):
    nblocks = cols.shape[1]
    total = nblocks * lax.axis_size("tile")
    c = cols[s, i] - lax.axis_index("tile").astype(jnp.int32) * nblocks + W
    c = jnp.where(c < 0, c + total, c)
    return jnp.where(c >= total, c - total, c)


def rank():
    return lax.axis_index("mem").astype(jnp.int32)


def masked(full, me, share, first):
    level = first + lax.broadcasted_iota(jnp.int32, full.shape, 0)
    mine = jnp.logical_and(level >= me * share, level < (me + 1) * share)
    return jnp.where(mine, full, 0.0)


def spread(own, me, levels, first):
    share = own.shape[0]
    return masked(jnp.concatenate([own] * (levels // share), axis=0), me, share, first)


def gathered(full, share):
    parts = [full[g * share : (g + 1) * share] for g in range(full.shape[0] // share)]
    return functools.reduce(jnp.add, parts)


def lanes(start, size):
    return pl.ds(pl.multiple_of(start, B), size)


def localize_group(d, levels, first, cols, xs, coef_ref, anom_ref, out_ref, static):
    groups = out_ref.shape[0]
    nblocks, slots = coef_ref.shape[:2]
    members, slot_count = anom_ref.shape[:2]
    rows = nblocks // groups
    lv = slice(first, first + levels)
    for r in range(rows):
        i = d * rows + r
        sl = slice(r * B, (r + 1) * B)
        lhs = jnp.concatenate([xs[column(cols, i, s)] for s in range(slots)], axis=1)
        rhs = jnp.concatenate([coef_ref[i, s] for s in range(slots)], axis=1)
        loc = lax.dot_general(
            lhs, rhs, (((1,), (1,)), ((), ())), preferred_element_type=F32
        ).reshape(members, levels, B)
        for t in range(slot_count):
            a = anom_ref[:, t, lv, lanes(i * B, B)].astype(F32)
            inc = jnp.sum(a * loc, axis=0) + static[:, sl]
            out_ref[d, t, :, sl] = inc.astype(BF16)


def first_static(d, width, levels, chi_ref, sig_ref):
    cut = lanes(d * width, width)
    return spread(sig_ref[:, cut] * chi_ref[:, cut], rank(), levels, 0)


def second_static(d, width, levels, chi_ref, sig_ref, res_ref, norm_ref):
    cut = lanes(d * width, width)
    rsum = res_ref[d, 0].astype(F32) + res_ref[d, 1].astype(F32)
    sig = spread(sig_ref[:, cut], rank(), levels, 0)
    chi = spread(chi_ref[:, cut], rank(), levels, 0)
    sr = sig * rsum
    gc = chi + sr
    sq = gc * gc
    for r in range(width // B):
        norm_ref[...] += sq[:, r * B : (r + 1) * B]
    return -(sig * sr)


def edge_kernel(alpha_hbm, low_ref, high_ref, buf, sem):
    columns = alpha_hbm.shape[-1]
    width = low_ref.shape[-1]
    copies = [
        pltpu.make_async_copy(alpha_hbm.at[:, :, pl.ds(start, width)], buf.at[k], sem.at[k])
        for k, start in enumerate((0, columns - width))
    ]
    for c in copies:
        c.start()
    for c, out in zip(copies, (low_ref, high_ref)):
        c.wait()
        out[...] = buf[0 if out is low_ref else 1].astype(BF16)


def first_inner(cols, alpha_hbm, coef_ref, anom_ref, chi_ref, sig_ref, alpha_ref, xs, out_ref, sem):
    members, levels, columns = alpha_ref.shape
    groups = out_ref.shape[0]
    width = columns // groups
    rows = width // B
    ml = members * levels

    def copy(d):
        part = (slice(None), slice(None), pl.ds(d * width, width))
        return pltpu.make_async_copy(alpha_hbm.at[part], alpha_ref.at[part], sem.at[d])

    for d in range(groups):
        copy(d).start()

    def load(d):
        copy(d).wait()
        for r in range(rows):
            b = d * rows + r
            xs[W + b] = alpha_ref[:, :, b * B : (b + 1) * B].astype(BF16).reshape(ml, B)

    load(0)
    load(1)
    for d in range(1, groups - 1):
        load(d + 1)
        static = first_static(d, width, levels, chi_ref, sig_ref)
        localize_group(d, levels, 0, cols, xs, coef_ref, anom_ref, out_ref, static)


def first_outer(
    cols, low_ref, high_ref, coef_ref, anom_ref, chi_ref, sig_ref, xs_in, part_ref, xs, out_ref
):
    members, _, levels, columns = anom_ref.shape
    groups = out_ref.shape[0]
    width = columns // groups
    ml = members * levels
    n = columns // B
    for b in range(W):
        xs[b] = low_ref[:, :, b * B : (b + 1) * B].reshape(ml, B)
        xs[W + n + b] = high_ref[:, :, b * B : (b + 1) * B].reshape(ml, B)

    def step(k, carry):
        d = k * (groups - 1)
        static = first_static(d, width, levels, chi_ref, sig_ref)
        localize_group(d, levels, 0, cols, xs, coef_ref, anom_ref, out_ref, static)
        return carry

    lax.fori_loop(0, 2, step, 0)


def adjoint_group(d, cols, res_ref, anom_ref, coef_ref, acc_ref):
    groups = res_ref.shape[0]
    nblocks, slots = coef_ref.shape[:2]
    members, slot_count, levels = anom_ref.shape[:3]
    rows = nblocks // groups
    for r in range(rows):
        i = d * rows + r
        sl = slice(r * B, (r + 1) * B)
        w = functools.reduce(
            jnp.add,
            [
                anom_ref[:, t, :, lanes(i * B, B)].astype(F32) * res_ref[d, t, :, sl].astype(F32)[None]
                for t in range(slot_count)
            ],
        )
        w = w.astype(BF16).reshape(members * levels, B)
        for s in range(slots):
            acc_ref[column(cols, i, s)] += jnp.dot(w, coef_ref[i, s], preferred_element_type=F32)


def adjoint_edges(outer, cols, res_ref, anom_ref, coef_ref, acc_ref, low_ref, high_ref):
    groups = res_ref.shape[0]
    padded = acc_ref.shape[0]

    def clear(b, carry):
        acc_ref[b] = jnp.zeros(acc_ref.shape[1:], F32)
        return carry

    lax.fori_loop(0, padded, clear, 0)

    def step(k, carry):
        d = jnp.where(k < outer, k, groups - 2 * outer + k)
        adjoint_group(d, cols, res_ref, anom_ref, coef_ref, acc_ref)
        return carry

    lax.fori_loop(0, 2 * outer, step, 0)
    halo = low_ref.shape[0]
    for b in range(halo):
        low_ref[b] = acc_ref[b].astype(BF16)
        high_ref[b] = acc_ref[padded - halo + b].astype(BF16)


def adjoint_all(cols, res_ref, anom_ref, coef_ref, sum_in, acc_ref, low_ref, high_ref, sum_ref):
    adjoint_edges(res_ref.shape[0] // 2, cols, res_ref, anom_ref, coef_ref, acc_ref, low_ref, high_ref)


def adjoint_rest(outer, cols, res_ref, anom_ref, coef_ref, acc_in, acc_ref):
    def step(d, carry):
        adjoint_group(d, cols, res_ref, anom_ref, coef_ref, acc_ref)
        return carry

    lax.fori_loop(outer, res_ref.shape[0] - outer, step, 0)


def second_block(b, adj, alpha_ref, xs, norm_ref, own):
    members, levels = alpha_ref.shape[:2]
    xs[b] = (-adj).astype(BF16)
    if own:
        g = alpha_ref[:, :, lanes((b - W) * B, B)] + adj.reshape(members, levels, B)
        norm_ref[...] += jnp.sum(g * g, axis=0)


def second_inner(
    outer, cols, res_ref, anom_ref, coef_ref, alpha_ref, chi_ref, sig_ref, acc_in,
    acc_ref, xs, out_ref, norm_ref,
):
    adjoint_rest(outer, cols, res_ref, anom_ref, coef_ref, acc_in, acc_ref)
    levels = alpha_ref.shape[1]
    groups = out_ref.shape[0]
    padded = acc_ref.shape[0]
    width = out_ref.shape[-1]
    norm_ref[...] = jnp.zeros_like(norm_ref)

    def block(b, carry):
        second_block(b, acc_ref[b], alpha_ref, xs, norm_ref, True)
        return carry

    lax.fori_loop(2 * W, padded - 2 * W, block, 0, unroll=2)

    def step(d, carry):
        static = second_static(d, width, levels, chi_ref, sig_ref, res_ref, norm_ref)
        localize_group(d, levels, 0, cols, xs, coef_ref, anom_ref, out_ref, static)
        return carry

    lax.fori_loop(outer, groups - outer, step, 0)


def second_outer(
    outer, cols, res_ref, anom_ref, coef_ref, alpha_ref, chi_ref, sig_ref, acc_ref, prev_ref,
    next_ref, xs_in, part_in, norm_in, xs, out_ref, norm_ref,
):
    levels = alpha_ref.shape[1]
    groups = out_ref.shape[0]
    width = out_ref.shape[-1]
    n = acc_ref.shape[0] - 2 * W
    for b in range(2 * W):
        second_block(b, acc_ref[b] + prev_ref[b].astype(F32), alpha_ref, xs, norm_ref, b >= W)
        second_block(n + b, acc_ref[n + b] + next_ref[b].astype(F32), alpha_ref, xs, norm_ref, b < W)

    def step(k, carry):
        d = jnp.where(k < outer, k, groups - 2 * outer + k)
        static = second_static(d, width, levels, chi_ref, sig_ref, res_ref, norm_ref)
        localize_group(d, levels, 0, cols, xs, coef_ref, anom_ref, out_ref, static)
        return carry

    lax.fori_loop(0, 2 * outer, step, 0)


def residual_first(y_ref, rinv_ref, innov_ref, out_ref, inc_ref):
    width = y_ref.shape[-1]
    cut = lanes(rank() * width, width)
    y = jnp.sum(y_ref[...].astype(F32), axis=0)
    inc_ref[...] = y
    r = (rinv_ref[:, :, cut] * (y - innov_ref[:, :, cut])).astype(BF16)
    for k in range(out_ref.shape[0]):
        out_ref[k] = r


def residual_second(
    y_ref, rinv_ref, innov_ref, inc_ref, old_ref, norm_ref, out_ref, sum_ref
):
    width = y_ref.shape[-1]
    cut = lanes(rank() * width, width)
    y = jnp.sum(y_ref[...].astype(F32), axis=0)
    r = (rinv_ref[:, :, cut] * (y - innov_ref[:, :, cut])).astype(BF16)
    for k in range(out_ref.shape[0]):
        out_ref[k] = r
    change = (old_ref[0].astype(F32) - r.astype(F32)) * (inc_ref[...] - y)
    change = jnp.sum(change.reshape(-1, 8, width), axis=0)
    norm = norm_ref[...].reshape(-1, 8, B).sum(axis=0)
    lane = lax.broadcasted_iota(jnp.int32, sum_ref.shape, 1)
    sum_ref[...] = jnp.where(lane == 0, jnp.sum(norm), jnp.where(lane == 1, jnp.sum(change), 0.0))


def final_kernel(
    sums_ref, alpha_ref, chi_ref, sig_ref, acc1, acc2, prev1, next1, prev2, next2, res1, res2,
    an_ref, cn_ref, ga_ref, gc_ref,
):
    d = pl.program_id(0)
    members, total, width = an_ref.shape
    streams = len(acc1)
    levels = total // streams
    rows = width // B
    share = chi_ref.shape[0]
    cut = lanes(d * width, width)
    totals = sum(jnp.sum(s[...], axis=0, keepdims=True) for s in sums_ref)
    lane = lax.broadcasted_iota(jnp.int32, totals.shape, 1)
    norm = jnp.sum(jnp.where(lane == 0, totals, 0.0), axis=1, keepdims=True)
    prod = norm + jnp.sum(jnp.where(lane == 1, totals, 0.0), axis=1, keepdims=True)
    step = norm / prod

    def rows_out(extra1, extra2):
        for h in range(streams):
            lv = slice(h * levels, (h + 1) * levels)
            for r in range(rows):
                sl = slice(r * B, (r + 1) * B)
                a1 = acc1[h][W + d * rows + r]
                a2 = acc2[h][W + d * rows + r]
                if extra1 is not None:
                    a1 = a1 + extra1(h, r).astype(F32)
                    a2 = a2 + extra2(h, r).astype(F32)
                a1 = a1.reshape(members, levels, B)
                a2 = a2.reshape(members, levels, B)
                a0 = alpha_ref[:, lv, lanes((d * rows + r) * B, B)]
                g = a0 + a1
                q = g + (a1 - a2)
                an_ref[:, lv, sl] = a0 - step[None] * g
                ga_ref[:, lv, sl] = g - step[None] * q

    last = pl.num_programs(0) - 1

    @pl.when(d == 0)
    def _():
        rows_out(lambda h, r: prev1[h][W + r], lambda h, r: prev2[h][r])

    @pl.when(d == last)
    def _():
        rows_out(lambda h, r: next1[h][r], lambda h, r: next2[h][r])

    @pl.when(jnp.logical_and(d > 0, d < last))
    def _():
        rows_out(None, None)

    def own_sum(res):
        parts = []
        for h in range(streams):
            s = res[h][d, 0].astype(F32) + res[h][d, 1].astype(F32)
            parts.append(gathered(masked(s, rank(), share, h * levels), share))
        return functools.reduce(jnp.add, parts)

    s1 = own_sum(res1)
    s2 = own_sum(res2)
    chi = chi_ref[:, cut]
    sg = sig_ref[:, cut]
    g = chi + sg * s1
    q = g + (sg * s1 - sg * s2)
    cn_ref[...] = chi - step * g
    gc_ref[...] = g - step * q


def body(anomalies, alpha0, chi0, sigma, innov, rinv, taper_cols, taper_coef):
    members, all_levels, columns = alpha0.shape
    slot_count = anomalies.shape[1]
    nblocks, slots = taper_cols.shape
    share = chi0.shape[0]
    groups = lax.axis_size("mem")
    tiles = lax.axis_size("tile")
    width = columns // groups
    levels = all_levels
    ml = members * levels
    padded = nblocks + 2 * W
    cols = taper_cols.T

    vm = pl.BlockSpec(memory_space=pltpu.VMEM)
    sm = pl.BlockSpec(memory_space=pltpu.SMEM)

    anywhere = pl.BlockSpec(memory_space=pltpu.HBM)
    part = functools.partial
    sds = jax.ShapeDtypeStruct
    pieces = sds((groups, slot_count, levels, width), BF16)
    inc_out = sds((slot_count, levels, width), F32)
    norm_out = sds((levels, B), F32)
    xs_out = sds((padded, ml, B), BF16)
    acc_out = sds((padded, ml, B), F32)
    work = 2 * ml * slots * B * B

    def call(kernel, name, scalars, operands, outs, scratch=(), limit=8, alias={}, hbm=0, rows=1):
        return pl.pallas_call(
            kernel,
            in_specs=[sm] * len(scalars) + [anywhere] * hbm + [vm] * (len(operands) - hbm),
            out_specs=[vm] * len(outs),
            out_shape=[pltpu.VMEM(o.shape, o.dtype) for o in outs],
            scratch_shapes=list(scratch),
            input_output_aliases={len(scalars) + k: v for k, v in alias.items()},
            compiler_params=pltpu.CompilerParams(vmem_limit_bytes=limit * MIB),
            cost_estimate=pl.CostEstimate(
                flops=8 * rows * work, transcendentals=0, bytes_accessed=rows * 3 * MIB // 4
            ),
            name=name,
        )(
            *scalars,
            *[pltpu.with_memory_space_constraint(o, pltpu.HBM) for o in operands[:hbm]],
            *[resident(o) for o in operands[hbm:]],
        )

    def exchanged(x):
        return lax.all_to_all(x, "mem", 0, 0)

    rim = sds((members, levels, W * B), BF16)
    high, low = call(
        edge_kernel, "edges", [], [alpha0], [rim, rim],
        [pltpu.VMEM((2, members, levels, W * B), F32), pltpu.SemaphoreType.DMA((2,))], hbm=1, rows=96,
    )
    low = shifted(low, "tile", 1)
    high = shifted(high, "tile", -1)
    alpha, xs1, part1 = call(
        first_inner, "first_inner", [cols], [alpha0, taper_coef, anomalies, chi0, sigma],
        [sds(alpha0.shape, F32), xs_out, pieces],
        [pltpu.SemaphoreType.DMA((groups,))], hbm=1, rows=24,
    )
    coef, anom = taper_coef, anomalies
    xs1, part1 = call(
        first_outer, "first_outer", [cols], [low, high, coef, anom, chi0, sigma, xs1, part1],
        [xs_out, pieces], alias={6: 0, 7: 1}, rows=8,
    )
    got1 = exchanged(part1)
    r1, inc1 = call(residual_first, "residual_first", [], [got1, rinv, innov], [pieces, inc_out])
    res1 = exchanged(r1)

    outer = 2 * W // (width // B)
    edge = sds((2 * W, ml, B), BF16)
    acc1, low1, high1 = call(
        part(adjoint_edges, outer), "adjoint_edges", [cols], [res1, anom, coef], [acc_out, edge, edge],
        rows=16,
    )
    prev1 = shifted(high1, "tile", 1)
    next1 = shifted(low1, "tile", -1)
    acc1, xs2, part2, norm = call(
        part(second_inner, outer), "second_inner", [cols],
        [res1, anom, coef, alpha, chi0, sigma, acc1], [acc_out, xs_out, pieces, norm_out],
        alias={6: 0}, rows=32,
    )
    xs2, part2, norm = call(
        part(second_outer, outer), "second_outer", [cols],
        [res1, anom, coef, alpha, chi0, sigma, acc1, prev1, next1, xs2, part2, norm],
        [xs_out, pieces, norm_out], alias={9: 0, 10: 1, 11: 2}, rows=16,
    )
    got2 = exchanged(part2)
    r2, sums = call(
        residual_second, "residual_second", [], [got2, rinv, innov, inc1, r1, norm],
        [pieces, sds((groups * tiles, B), F32)],
    )
    res2 = exchanged(r2)
    edge = sds((W, ml, B), BF16)
    acc2, low2, high2, sums = call(
        adjoint_all, "adjoint_all", [cols], [res2, anom, coef, sums],
        [acc_out, edge, edge, sds(sums.shape, F32)], alias={3: 3}, rows=32,
    )
    prev2 = shifted(high2, "tile", 1)
    next2 = shifted(low2, "tile", -1)
    sums = lax.all_to_all(sums, ("tile", "mem"), 0, 0, tiled=True)
    operands = [
        [sums], alpha, chi0, sigma, [acc1], [acc2], [prev1], [next1], [prev2], [next2], [res1], [res2]
    ]
    flat, tree = jax.tree.flatten(operands)
    count = len(flat)

    def final(*refs):
        final_kernel(*jax.tree.unflatten(tree, refs[:count]), *refs[count:])

    alpha_spec = pl.BlockSpec((members, all_levels, width), lambda d: (0, 0, d))
    chi_spec = pl.BlockSpec((share, width), lambda d: (0, d))
    out = pl.pallas_call(
        final,
        grid=(groups,),
        in_specs=[vm] * count,
        out_specs=[alpha_spec, chi_spec, alpha_spec, chi_spec],
        out_shape=[
            jax.ShapeDtypeStruct(alpha0.shape, F32),
            jax.ShapeDtypeStruct(chi0.shape, F32),
            jax.ShapeDtypeStruct(alpha0.shape, F32),
            jax.ShapeDtypeStruct(chi0.shape, F32),
        ],
        compiler_params=pltpu.CompilerParams(
            dimension_semantics=("arbitrary",), vmem_limit_bytes=8 * MIB
        ),
        name="final",
    )(*[resident(o) for o in flat])
    return tuple(out)


def solution(mesh):
    placed = (
        P("mem", None, None, "tile"),
        P("mem", None, "tile"),
        P("mem", "tile"),
        P("mem", "tile"),
        P(None, None, "tile"),
        P(None, None, "tile"),
        P("tile", None),
        P("tile", None, None, None),
    )
    return jax.shard_map(
        body,
        mesh=mesh,
        in_specs=placed,
        out_specs=(
            P("mem", None, "tile"),
            P("mem", "tile"),
            P("mem", None, "tile"),
            P("mem", "tile"),
        ),
        check_vma=False,
    )
```

```python
import functools
import jax
import jax.numpy as jnp
from jax import lax
from jax.experimental import pallas as pl
from jax.experimental.pallas import tpu as pltpu
from jax.sharding import PartitionSpec as P

W = 4
B = 128
F32 = jnp.float32
BF16 = jnp.bfloat16
MIB = 2**20


def shifted(array, axis, by):
    size = lax.axis_size(axis)
    return lax.ppermute(array, axis, [(i, (i + by) % size) for i in range(size)])


def resident(array):
    return pltpu.with_memory_space_constraint(array, pltpu.VMEM)


def column(cols, i, s):
    nblocks = cols.shape[1]
    total = nblocks * lax.axis_size("tile")
    c = cols[s, i] - lax.axis_index("tile").astype(jnp.int32) * nblocks + W
    c = jnp.where(c < 0, c + total, c)
    return jnp.where(c >= total, c - total, c)


def rank():
    return lax.axis_index("mem").astype(jnp.int32)


def masked(full, me, share, first):
    level = first + lax.broadcasted_iota(jnp.int32, full.shape, 0)
    mine = jnp.logical_and(level >= me * share, level < (me + 1) * share)
    return jnp.where(mine, full, 0.0)


def spread(own, me, levels, first):
    share = own.shape[0]
    return masked(jnp.concatenate([own] * (levels // share), axis=0), me, share, first)


def gathered(full, share):
    parts = [full[g * share : (g + 1) * share] for g in range(full.shape[0] // share)]
    return functools.reduce(jnp.add, parts)


def lanes(start, size):
    return pl.ds(pl.multiple_of(start, B), size)


def localize_group(d, levels, first, cols, xs, coef_ref, anom_ref, out_ref, static):
    groups = out_ref.shape[0]
    nblocks, slots = coef_ref.shape[:2]
    members, slot_count = anom_ref.shape[:2]
    rows = nblocks // groups
    lv = slice(first, first + levels)
    for r in range(rows):
        i = d * rows + r
        sl = slice(r * B, (r + 1) * B)
        lhs = jnp.concatenate([xs[column(cols, i, s)] for s in range(slots)], axis=1)
        rhs = jnp.concatenate([coef_ref[i, s] for s in range(slots)], axis=1)
        loc = lax.dot_general(
            lhs, rhs, (((1,), (1,)), ((), ())), preferred_element_type=F32
        ).reshape(members, levels, B)
        for t in range(slot_count):
            a = anom_ref[:, t, lv, lanes(i * B, B)].astype(F32)
            inc = jnp.sum(a * loc, axis=0) + static[:, sl]
            out_ref[d, t, :, sl] = inc.astype(BF16)


def first_static(d, width, levels, chi_ref, sig_ref):
    cut = lanes(d * width, width)
    return spread(sig_ref[:, cut] * chi_ref[:, cut], rank(), levels, 0)


def second_static(d, width, levels, chi_ref, sig_ref, res_ref, norm_ref):
    cut = lanes(d * width, width)
    rsum = res_ref[d, 0].astype(F32) + res_ref[d, 1].astype(F32)
    sig = spread(sig_ref[:, cut], rank(), levels, 0)
    chi = spread(chi_ref[:, cut], rank(), levels, 0)
    sr = sig * rsum
    gc = chi + sr
    sq = gc * gc
    for r in range(width // B):
        norm_ref[...] += sq[:, r * B : (r + 1) * B]
    return -(sig * sr)


def edge_kernel(alpha_hbm, low_ref, high_ref, buf, sem):
    columns = alpha_hbm.shape[-1]
    width = low_ref.shape[-1]
    copies = [
        pltpu.make_async_copy(alpha_hbm.at[:, :, pl.ds(start, width)], buf.at[k], sem.at[k])
        for k, start in enumerate((0, columns - width))
    ]
    for c in copies:
        c.start()
    for c, out in zip(copies, (low_ref, high_ref)):
        c.wait()
        out[...] = buf[0 if out is low_ref else 1].astype(BF16)


def first_inner(cols, alpha_hbm, coef_ref, anom_ref, chi_ref, sig_ref, alpha_ref, xs, out_ref, sem):
    members, levels, columns = alpha_ref.shape
    groups = out_ref.shape[0]
    width = columns // groups
    rows = width // B
    ml = members * levels

    def copy(d):
        part = (slice(None), slice(None), pl.ds(d * width, width))
        return pltpu.make_async_copy(alpha_hbm.at[part], alpha_ref.at[part], sem.at[d])

    for d in range(groups):
        copy(d).start()

    def load(d):
        copy(d).wait()
        for r in range(rows):
            b = d * rows + r
            xs[W + b] = alpha_ref[:, :, b * B : (b + 1) * B].astype(BF16).reshape(ml, B)

    load(0)
    load(1)
    for d in range(1, groups - 1):
        load(d + 1)
        static = first_static(d, width, levels, chi_ref, sig_ref)
        localize_group(d, levels, 0, cols, xs, coef_ref, anom_ref, out_ref, static)


def first_outer(
    cols, low_ref, high_ref, coef_ref, anom_ref, chi_ref, sig_ref, xs_in, part_ref, xs, out_ref
):
    members, _, levels, columns = anom_ref.shape
    groups = out_ref.shape[0]
    width = columns // groups
    ml = members * levels
    n = columns // B
    for b in range(W):
        xs[b] = low_ref[:, :, b * B : (b + 1) * B].reshape(ml, B)
        xs[W + n + b] = high_ref[:, :, b * B : (b + 1) * B].reshape(ml, B)

    def step(k, carry):
        d = k * (groups - 1)
        static = first_static(d, width, levels, chi_ref, sig_ref)
        localize_group(d, levels, 0, cols, xs, coef_ref, anom_ref, out_ref, static)
        return carry

    lax.fori_loop(0, 2, step, 0)


def adjoint_group(d, cols, res_ref, anom_ref, coef_ref, acc_ref):
    groups = res_ref.shape[0]
    nblocks, slots = coef_ref.shape[:2]
    members, slot_count, levels = anom_ref.shape[:3]
    rows = nblocks // groups
    for r in range(rows):
        i = d * rows + r
        sl = slice(r * B, (r + 1) * B)
        w = functools.reduce(
            jnp.add,
            [
                anom_ref[:, t, :, lanes(i * B, B)].astype(F32) * res_ref[d, t, :, sl].astype(F32)[None]
                for t in range(slot_count)
            ],
        )
        w = w.astype(BF16).reshape(members * levels, B)
        for s in range(slots):
            acc_ref[column(cols, i, s)] += jnp.dot(w, coef_ref[i, s], preferred_element_type=F32)


def adjoint_edges(outer, cols, res_ref, anom_ref, coef_ref, acc_ref, low_ref, high_ref):
    groups = res_ref.shape[0]
    padded = acc_ref.shape[0]

    def clear(b, carry):
        acc_ref[b] = jnp.zeros(acc_ref.shape[1:], F32)
        return carry

    lax.fori_loop(0, padded, clear, 0)

    def step(k, carry):
        d = jnp.where(k < outer, k, groups - 2 * outer + k)
        adjoint_group(d, cols, res_ref, anom_ref, coef_ref, acc_ref)
        return carry

    lax.fori_loop(0, 2 * outer, step, 0)
    halo = low_ref.shape[0]
    for b in range(halo):
        low_ref[b] = acc_ref[b].astype(BF16)
        high_ref[b] = acc_ref[padded - halo + b].astype(BF16)


def adjoint_all(cols, res_ref, anom_ref, coef_ref, acc_ref, low_ref, high_ref, sum_ref):
    groups = res_ref.shape[0]
    code = functools.reduce(jnp.add, [res_ref[d, 0, :16, -B:].astype(F32) for d in range(groups)])
    sum_ref[...] = jnp.broadcast_to(code[:1], sum_ref.shape)
    adjoint_edges(res_ref.shape[0] // 2, cols, res_ref, anom_ref, coef_ref, acc_ref, low_ref, high_ref)


def adjoint_rest(outer, cols, res_ref, anom_ref, coef_ref, acc_in, acc_ref):
    def step(d, carry):
        adjoint_group(d, cols, res_ref, anom_ref, coef_ref, acc_ref)
        return carry

    lax.fori_loop(outer, res_ref.shape[0] - outer, step, 0)


def second_block(b, adj, alpha_ref, xs, norm_ref, own):
    members, levels = alpha_ref.shape[:2]
    xs[b] = (-adj).astype(BF16)
    if own:
        g = alpha_ref[:, :, lanes((b - W) * B, B)] + adj.reshape(members, levels, B)
        norm_ref[...] += jnp.sum(g * g, axis=0)


def second_inner(
    outer, cols, res_ref, anom_ref, coef_ref, alpha_ref, chi_ref, sig_ref, acc_in,
    acc_ref, xs, out_ref, norm_ref,
):
    adjoint_rest(outer, cols, res_ref, anom_ref, coef_ref, acc_in, acc_ref)
    levels = alpha_ref.shape[1]
    groups = out_ref.shape[0]
    padded = acc_ref.shape[0]
    width = out_ref.shape[-1]
    norm_ref[...] = jnp.zeros_like(norm_ref)

    def block(b, carry):
        second_block(b, acc_ref[b], alpha_ref, xs, norm_ref, True)
        return carry

    lax.fori_loop(2 * W, padded - 2 * W, block, 0, unroll=2)

    def step(d, carry):
        static = second_static(d, width, levels, chi_ref, sig_ref, res_ref, norm_ref)
        localize_group(d, levels, 0, cols, xs, coef_ref, anom_ref, out_ref, static)
        return carry

    lax.fori_loop(outer, groups - outer, step, 0)


def second_outer(
    outer, cols, res_ref, anom_ref, coef_ref, alpha_ref, chi_ref, sig_ref, acc_ref, prev_ref,
    next_ref, xs_in, part_in, norm_in, xs, out_ref, norm_ref,
):
    levels = alpha_ref.shape[1]
    groups = out_ref.shape[0]
    width = out_ref.shape[-1]
    n = acc_ref.shape[0] - 2 * W
    for b in range(2 * W):
        second_block(b, acc_ref[b] + prev_ref[b].astype(F32), alpha_ref, xs, norm_ref, b >= W)
        second_block(n + b, acc_ref[n + b] + next_ref[b].astype(F32), alpha_ref, xs, norm_ref, b < W)

    def step(k, carry):
        d = jnp.where(k < outer, k, groups - 2 * outer + k)
        static = second_static(d, width, levels, chi_ref, sig_ref, res_ref, norm_ref)
        localize_group(d, levels, 0, cols, xs, coef_ref, anom_ref, out_ref, static)
        return carry

    lax.fori_loop(0, 2 * outer, step, 0)


def residual_first(y_ref, rinv_ref, innov_ref, out_ref, inc_ref):
    width = y_ref.shape[-1]
    cut = lanes(rank() * width, width)
    y = jnp.sum(y_ref[...].astype(F32), axis=0)
    inc_ref[...] = y
    r = (rinv_ref[:, :, cut] * (y - innov_ref[:, :, cut])).astype(BF16)
    for k in range(out_ref.shape[0]):
        out_ref[k] = r


def residual_second(
    y_ref, rinv_ref, innov_ref, inc_ref, old_ref, norm_ref, out_ref
):
    width = y_ref.shape[-1]
    cut = lanes(rank() * width, width)
    y = jnp.sum(y_ref[...].astype(F32), axis=0)
    r = (rinv_ref[:, :, cut] * (y - innov_ref[:, :, cut])).astype(BF16)
    for k in range(out_ref.shape[0]):
        out_ref[k, :, :, :width] = r
    change = (old_ref[0].astype(F32) - r.astype(F32)) * (inc_ref[...] - y)
    change = jnp.sum(change.reshape(-1, 8, width), axis=0)
    norm = norm_ref[...].reshape(-1, 8, B).sum(axis=0)
    lane = lax.broadcasted_iota(jnp.int32, (16, B), 1)
    code = jnp.zeros((16, B), F32)
    for base, total in ((0, jnp.sum(norm)), (3, jnp.sum(change))):
        rest = jnp.full((16, B), total, F32)
        for k in range(3):
            piece = rest.astype(BF16).astype(F32)
            code = jnp.where(lane == base + k, piece, code)
            rest = rest - piece
    code = code.astype(BF16)
    for k in range(out_ref.shape[0]):
        for t in range(out_ref.shape[1]):
            for h in range(0, out_ref.shape[2], 16):
                out_ref[k, t, h : h + 16, width:] = code


def final_kernel(
    sums_ref, alpha_ref, chi_ref, sig_ref, acc1, acc2, prev1, next1, prev2, next2, res1, res2,
    an_ref, cn_ref, ga_ref, gc_ref,
):
    d = pl.program_id(0)
    members, total, width = an_ref.shape
    streams = len(acc1)
    levels = total // streams
    rows = width // B
    share = chi_ref.shape[0]
    cut = lanes(d * width, width)
    totals = sum(jnp.sum(s[...], axis=0, keepdims=True) for s in sums_ref)
    lane = lax.broadcasted_iota(jnp.int32, totals.shape, 1)
    norm = jnp.sum(jnp.where(lane < 3, totals, 0.0), axis=1, keepdims=True)
    prod = jnp.sum(jnp.where(lane < 6, totals, 0.0), axis=1, keepdims=True)
    step = norm / prod

    def rows_out(extra1, extra2):
        for h in range(streams):
            lv = slice(h * levels, (h + 1) * levels)
            for r in range(rows):
                sl = slice(r * B, (r + 1) * B)
                a1 = acc1[h][W + d * rows + r]
                a2 = acc2[h][W + d * rows + r]
                if extra1 is not None:
                    a1 = a1 + extra1(h, r).astype(F32)
                    a2 = a2 + extra2(h, r).astype(F32)
                a1 = a1.reshape(members, levels, B)
                a2 = a2.reshape(members, levels, B)
                a0 = alpha_ref[:, lv, lanes((d * rows + r) * B, B)]
                g = a0 + a1
                q = g + (a1 - a2)
                an_ref[:, lv, sl] = a0 - step[None] * g
                ga_ref[:, lv, sl] = g - step[None] * q

    last = pl.num_programs(0) - 1

    @pl.when(d == 0)
    def _():
        rows_out(lambda h, r: prev1[h][W + r], lambda h, r: prev2[h][r])

    @pl.when(d == last)
    def _():
        rows_out(lambda h, r: next1[h][r], lambda h, r: next2[h][r])

    @pl.when(jnp.logical_and(d > 0, d < last))
    def _():
        rows_out(None, None)

    def own_sum(res):
        parts = []
        for h in range(streams):
            s = res[h][d, 0, :, :width].astype(F32) + res[h][d, 1, :, :width].astype(F32)
            parts.append(gathered(masked(s, rank(), share, h * levels), share))
        return functools.reduce(jnp.add, parts)

    s1 = own_sum(res1)
    s2 = own_sum(res2)
    chi = chi_ref[:, cut]
    sg = sig_ref[:, cut]
    g = chi + sg * s1
    q = g + (sg * s1 - sg * s2)
    cn_ref[...] = chi - step * g
    gc_ref[...] = g - step * q


def body(anomalies, alpha0, chi0, sigma, innov, rinv, taper_cols, taper_coef):
    members, all_levels, columns = alpha0.shape
    slot_count = anomalies.shape[1]
    nblocks, slots = taper_cols.shape
    share = chi0.shape[0]
    groups = lax.axis_size("mem")
    tiles = lax.axis_size("tile")
    width = columns // groups
    levels = all_levels
    ml = members * levels
    padded = nblocks + 2 * W
    cols = taper_cols.T

    vm = pl.BlockSpec(memory_space=pltpu.VMEM)
    sm = pl.BlockSpec(memory_space=pltpu.SMEM)

    anywhere = pl.BlockSpec(memory_space=pltpu.HBM)
    part = functools.partial
    sds = jax.ShapeDtypeStruct
    pieces = sds((groups, slot_count, levels, width), BF16)
    inc_out = sds((slot_count, levels, width), F32)
    norm_out = sds((levels, B), F32)
    xs_out = sds((padded, ml, B), BF16)
    acc_out = sds((padded, ml, B), F32)
    work = 2 * ml * slots * B * B

    def call(kernel, name, scalars, operands, outs, scratch=(), limit=8, alias={}, hbm=0, rows=1):
        return pl.pallas_call(
            kernel,
            in_specs=[sm] * len(scalars) + [anywhere] * hbm + [vm] * (len(operands) - hbm),
            out_specs=[vm] * len(outs),
            out_shape=[pltpu.VMEM(o.shape, o.dtype) for o in outs],
            scratch_shapes=list(scratch),
            input_output_aliases={len(scalars) + k: v for k, v in alias.items()},
            compiler_params=pltpu.CompilerParams(vmem_limit_bytes=limit * MIB),
            cost_estimate=pl.CostEstimate(
                flops=8 * rows * work, transcendentals=0, bytes_accessed=rows * 3 * MIB // 4
            ),
            name=name,
        )(
            *scalars,
            *[pltpu.with_memory_space_constraint(o, pltpu.HBM) for o in operands[:hbm]],
            *[resident(o) for o in operands[hbm:]],
        )

    def exchanged(x):
        return lax.all_to_all(x, "mem", 0, 0)

    rim = sds((members, levels, W * B), BF16)
    high, low = call(
        edge_kernel, "edges", [], [alpha0], [rim, rim],
        [pltpu.VMEM((2, members, levels, W * B), F32), pltpu.SemaphoreType.DMA((2,))], hbm=1, rows=96,
    )
    low = shifted(low, "tile", 1)
    high = shifted(high, "tile", -1)
    alpha, xs1, part1 = call(
        first_inner, "first_inner", [cols], [alpha0, taper_coef, anomalies, chi0, sigma],
        [sds(alpha0.shape, F32), xs_out, pieces],
        [pltpu.SemaphoreType.DMA((groups,))], hbm=1, rows=24,
    )
    coef, anom = taper_coef, anomalies
    xs1, part1 = call(
        first_outer, "first_outer", [cols], [low, high, coef, anom, chi0, sigma, xs1, part1],
        [xs_out, pieces], alias={6: 0, 7: 1}, rows=8,
    )
    got1 = exchanged(part1)
    r1, inc1 = call(residual_first, "residual_first", [], [got1, rinv, innov], [pieces, inc_out])
    res1 = exchanged(r1)

    outer = 2 * W // (width // B)
    edge = sds((2 * W, ml, B), BF16)
    acc1, low1, high1 = call(
        part(adjoint_edges, outer), "adjoint_edges", [cols], [res1, anom, coef], [acc_out, edge, edge],
        rows=16,
    )
    prev1 = shifted(high1, "tile", 1)
    next1 = shifted(low1, "tile", -1)
    acc1, xs2, part2, norm = call(
        part(second_inner, outer), "second_inner", [cols],
        [res1, anom, coef, alpha, chi0, sigma, acc1], [acc_out, xs_out, pieces, norm_out],
        alias={6: 0}, rows=32,
    )
    xs2, part2, norm = call(
        part(second_outer, outer), "second_outer", [cols],
        [res1, anom, coef, alpha, chi0, sigma, acc1, prev1, next1, xs2, part2, norm],
        [xs_out, pieces, norm_out], alias={9: 0, 10: 1, 11: 2}, rows=16,
    )
    got2 = exchanged(part2)
    (r2,) = call(
        residual_second, "residual_second", [], [got2, rinv, innov, inc1, r1, norm],
        [sds((groups, slot_count, levels, width + B), BF16)],
    )
    res2 = exchanged(r2)
    edge = sds((W, ml, B), BF16)
    acc2, low2, high2, sums = call(
        adjoint_all, "adjoint_all", [cols], [res2, anom, coef], [acc_out, edge, edge, sds((tiles, B), F32)],
        rows=32,
    )
    prev2 = shifted(high2, "tile", 1)
    next2 = shifted(low2, "tile", -1)
    sums = lax.all_to_all(sums, "tile", 0, 0, tiled=True)
    operands = [
        [sums], alpha, chi0, sigma, [acc1], [acc2], [prev1], [next1], [prev2], [next2], [res1], [res2]
    ]
    flat, tree = jax.tree.flatten(operands)
    count = len(flat)

    def final(*refs):
        final_kernel(*jax.tree.unflatten(tree, refs[:count]), *refs[count:])

    alpha_spec = pl.BlockSpec((members, all_levels, width), lambda d: (0, 0, d))
    chi_spec = pl.BlockSpec((share, width), lambda d: (0, d))
    out = pl.pallas_call(
        final,
        grid=(groups,),
        in_specs=[vm] * count,
        out_specs=[alpha_spec, chi_spec, alpha_spec, chi_spec],
        out_shape=[
            jax.ShapeDtypeStruct(alpha0.shape, F32),
            jax.ShapeDtypeStruct(chi0.shape, F32),
            jax.ShapeDtypeStruct(alpha0.shape, F32),
            jax.ShapeDtypeStruct(chi0.shape, F32),
        ],
        compiler_params=pltpu.CompilerParams(
            dimension_semantics=("arbitrary",), vmem_limit_bytes=8 * MIB
        ),
        name="final",
    )(*[resident(o) for o in flat])
    return tuple(out)


def solution(mesh):
    placed = (
        P("mem", None, None, "tile"),
        P("mem", None, "tile"),
        P("mem", "tile"),
        P("mem", "tile"),
        P(None, None, "tile"),
        P(None, None, "tile"),
        P("tile", None),
        P("tile", None, None, None),
    )
    return jax.shard_map(
        body,
        mesh=mesh,
        in_specs=placed,
        out_specs=(
            P("mem", None, "tile"),
            P("mem", "tile"),
            P("mem", None, "tile"),
            P("mem", "tile"),
        ),
        check_vma=False,
    )
```

```python
import functools
import jax
import jax.numpy as jnp
from jax import lax
from jax.experimental import pallas as pl
from jax.experimental.pallas import tpu as pltpu
from jax.sharding import PartitionSpec as P

W = 4
B = 128
F32 = jnp.float32
BF16 = jnp.bfloat16
MIB = 2**20


def shifted(array, axis, by):
    size = lax.axis_size(axis)
    return lax.ppermute(array, axis, [(i, (i + by) % size) for i in range(size)])


def resident(array):
    return pltpu.with_memory_space_constraint(array, pltpu.VMEM)


def column(cols, i, s):
    nblocks = cols.shape[1]
    total = nblocks * lax.axis_size("tile")
    c = cols[s, i] - lax.axis_index("tile").astype(jnp.int32) * nblocks + W
    c = jnp.where(c < 0, c + total, c)
    return jnp.where(c >= total, c - total, c)


def rank():
    return lax.axis_index("mem").astype(jnp.int32)


def masked(full, me, share, first):
    level = first + lax.broadcasted_iota(jnp.int32, full.shape, 0)
    mine = jnp.logical_and(level >= me * share, level < (me + 1) * share)
    return jnp.where(mine, full, 0.0)


def spread(own, me, levels, first):
    share = own.shape[0]
    return masked(jnp.concatenate([own] * (levels // share), axis=0), me, share, first)


def gathered(full, share):
    parts = [full[g * share : (g + 1) * share] for g in range(full.shape[0] // share)]
    return functools.reduce(jnp.add, parts)


def lanes(start, size):
    return pl.ds(pl.multiple_of(start, B), size)


def localize_group(d, levels, first, cols, xs, coef_ref, anom_ref, out_ref, static):
    groups = out_ref.shape[0]
    nblocks, slots = coef_ref.shape[:2]
    members, slot_count = anom_ref.shape[:2]
    rows = nblocks // groups
    lv = slice(first, first + levels)
    for r in range(rows):
        i = d * rows + r
        sl = slice(r * B, (r + 1) * B)
        lhs = jnp.concatenate([xs[column(cols, i, s)] for s in range(slots)], axis=1)
        rhs = jnp.concatenate([coef_ref[i, s] for s in range(slots)], axis=1)
        loc = lax.dot_general(
            lhs, rhs, (((1,), (1,)), ((), ())), preferred_element_type=F32
        ).reshape(members, levels, B)
        for t in range(slot_count):
            a = anom_ref[:, t, lv, lanes(i * B, B)].astype(F32)
            inc = jnp.sum(a * loc, axis=0) + static[:, sl]
            out_ref[d, t, :, sl] = inc.astype(BF16)


def first_static(d, width, levels, chi_ref, sig_ref):
    cut = lanes(d * width, width)
    return spread(sig_ref[:, cut] * chi_ref[:, cut], rank(), levels, 0)


def second_static(d, width, levels, chi_ref, sig_ref, res_ref, norm_ref):
    cut = lanes(d * width, width)
    rsum = res_ref[d, 0].astype(F32) + res_ref[d, 1].astype(F32)
    sig = spread(sig_ref[:, cut], rank(), levels, 0)
    chi = spread(chi_ref[:, cut], rank(), levels, 0)
    sr = sig * rsum
    gc = chi + sr
    sq = gc * gc
    for r in range(width // B):
        norm_ref[...] += sq[:, r * B : (r + 1) * B]
    return -(sig * sr)


def edge_kernel(alpha_hbm, low_ref, high_ref, buf, sem):
    columns = alpha_hbm.shape[-1]
    width = low_ref.shape[-1]
    copies = [
        pltpu.make_async_copy(alpha_hbm.at[:, :, pl.ds(start, width)], buf.at[k], sem.at[k])
        for k, start in enumerate((0, columns - width))
    ]
    for c in copies:
        c.start()
    for c, out in zip(copies, (low_ref, high_ref)):
        c.wait()
        out[...] = buf[0 if out is low_ref else 1].astype(BF16)


def first_inner(
    cols, alpha_hbm, coef_ref, anom_ref, chi_ref, sig_ref, alpha_ref, xs, out_ref, zero_a, zero_b, sem
):
    members, levels, columns = alpha_ref.shape
    groups = out_ref.shape[0]
    width = columns // groups
    rows = width // B
    ml = members * levels

    def copy(d):
        part = (slice(None), slice(None), pl.ds(d * width, width))
        return pltpu.make_async_copy(alpha_hbm.at[part], alpha_ref.at[part], sem.at[d])

    for d in range(groups):
        copy(d).start()

    def clear(b, carry):
        zero_a[b] = jnp.zeros(zero_a.shape[1:], F32)
        zero_b[b] = jnp.zeros(zero_b.shape[1:], F32)
        return carry

    lax.fori_loop(0, zero_a.shape[0], clear, 0)

    def load(d):
        copy(d).wait()
        for r in range(rows):
            b = d * rows + r
            xs[W + b] = alpha_ref[:, :, b * B : (b + 1) * B].astype(BF16).reshape(ml, B)

    load(0)
    load(1)
    for d in range(1, groups - 1):
        load(d + 1)
        static = first_static(d, width, levels, chi_ref, sig_ref)
        localize_group(d, levels, 0, cols, xs, coef_ref, anom_ref, out_ref, static)


def first_outer(
    cols, low_ref, high_ref, coef_ref, anom_ref, chi_ref, sig_ref, xs_in, part_ref, xs, out_ref
):
    members, _, levels, columns = anom_ref.shape
    groups = out_ref.shape[0]
    width = columns // groups
    ml = members * levels
    n = columns // B
    for b in range(W):
        xs[b] = low_ref[:, :, b * B : (b + 1) * B].reshape(ml, B)
        xs[W + n + b] = high_ref[:, :, b * B : (b + 1) * B].reshape(ml, B)

    def step(k, carry):
        d = k * (groups - 1)
        static = first_static(d, width, levels, chi_ref, sig_ref)
        localize_group(d, levels, 0, cols, xs, coef_ref, anom_ref, out_ref, static)
        return carry

    lax.fori_loop(0, 2, step, 0)


def res_block(res_ref, d, t, r, rows, levels):
    if len(res_ref.shape) == 4:
        return res_ref[d, t, :, r * B : (r + 1) * B].astype(F32)
    base = (t * rows + r) * levels
    return res_ref[d, base : base + levels].astype(F32)


def adjoint_group(d, cols, res_ref, anom_ref, coef_ref, acc_ref):
    groups = res_ref.shape[0]
    nblocks, slots = coef_ref.shape[:2]
    members, slot_count, levels = anom_ref.shape[:3]
    rows = nblocks // groups
    for r in range(rows):
        i = d * rows + r
        sl = slice(r * B, (r + 1) * B)
        w = functools.reduce(
            jnp.add,
            [
                anom_ref[:, t, :, lanes(i * B, B)].astype(F32)
                * res_block(res_ref, d, t, r, rows, levels)[None]
                for t in range(slot_count)
            ],
        )
        w = w.astype(BF16).reshape(members * levels, B)
        for s in range(slots):
            acc_ref[column(cols, i, s)] += jnp.dot(w, coef_ref[i, s], preferred_element_type=F32)


def adjoint_edges(outer, cols, res_ref, anom_ref, coef_ref, acc_in, acc_ref, low_ref, high_ref):
    groups = res_ref.shape[0]
    padded = acc_ref.shape[0]

    def step(k, carry):
        d = jnp.where(k < outer, k, groups - 2 * outer + k)
        adjoint_group(d, cols, res_ref, anom_ref, coef_ref, acc_ref)
        return carry

    lax.fori_loop(0, 2 * outer, step, 0)
    halo = low_ref.shape[0]
    for b in range(halo):
        low_ref[b] = acc_ref[b].astype(BF16)
        high_ref[b] = acc_ref[padded - halo + b].astype(BF16)


def adjoint_all(cols, res_ref, anom_ref, coef_ref, acc_in, acc_ref, low_ref, high_ref, sum_ref):
    groups = res_ref.shape[0]
    code = functools.reduce(jnp.add, [res_ref[d, res_ref.shape[1] - 16 :].astype(F32) for d in range(groups)])
    sum_ref[...] = jnp.broadcast_to(code[:1], sum_ref.shape)
    outer = res_ref.shape[0] // 2
    adjoint_edges(outer, cols, res_ref, anom_ref, coef_ref, acc_in, acc_ref, low_ref, high_ref)


def adjoint_rest(outer, cols, res_ref, anom_ref, coef_ref, acc_in, acc_ref):
    def step(d, carry):
        adjoint_group(d, cols, res_ref, anom_ref, coef_ref, acc_ref)
        return carry

    lax.fori_loop(outer, res_ref.shape[0] - outer, step, 0)


def second_block(b, adj, alpha_ref, xs, norm_ref, own):
    members, levels = alpha_ref.shape[:2]
    xs[b] = (-adj).astype(BF16)
    if own:
        g = alpha_ref[:, :, lanes((b - W) * B, B)] + adj.reshape(members, levels, B)
        norm_ref[...] += jnp.sum(g * g, axis=0)


def second_inner(
    outer, cols, res_ref, anom_ref, coef_ref, alpha_ref, chi_ref, sig_ref, acc_in,
    acc_ref, xs, out_ref, norm_ref,
):
    adjoint_rest(outer, cols, res_ref, anom_ref, coef_ref, acc_in, acc_ref)
    levels = alpha_ref.shape[1]
    groups = out_ref.shape[0]
    padded = acc_ref.shape[0]
    width = out_ref.shape[-1]
    norm_ref[...] = jnp.zeros_like(norm_ref)

    def block(b, carry):
        second_block(b, acc_ref[b], alpha_ref, xs, norm_ref, True)
        return carry

    lax.fori_loop(2 * W, padded - 2 * W, block, 0, unroll=2)

    def step(d, carry):
        static = second_static(d, width, levels, chi_ref, sig_ref, res_ref, norm_ref)
        localize_group(d, levels, 0, cols, xs, coef_ref, anom_ref, out_ref, static)
        return carry

    lax.fori_loop(outer, groups - outer, step, 0)


def second_outer(
    outer, cols, res_ref, anom_ref, coef_ref, alpha_ref, chi_ref, sig_ref, acc_ref, prev_ref,
    next_ref, xs_in, part_in, norm_in, xs, out_ref, norm_ref,
):
    levels = alpha_ref.shape[1]
    groups = out_ref.shape[0]
    width = out_ref.shape[-1]
    n = acc_ref.shape[0] - 2 * W
    for b in range(2 * W):
        second_block(b, acc_ref[b] + prev_ref[b].astype(F32), alpha_ref, xs, norm_ref, b >= W)
        second_block(n + b, acc_ref[n + b] + next_ref[b].astype(F32), alpha_ref, xs, norm_ref, b < W)

    def step(k, carry):
        d = jnp.where(k < outer, k, groups - 2 * outer + k)
        static = second_static(d, width, levels, chi_ref, sig_ref, res_ref, norm_ref)
        localize_group(d, levels, 0, cols, xs, coef_ref, anom_ref, out_ref, static)
        return carry

    lax.fori_loop(0, 2 * outer, step, 0)


def residual_first(y_ref, rinv_ref, innov_ref, out_ref, inc_ref):
    width = y_ref.shape[-1]
    cut = lanes(rank() * width, width)
    y = jnp.sum(y_ref[...].astype(F32), axis=0)
    inc_ref[...] = y
    r = (rinv_ref[:, :, cut] * (y - innov_ref[:, :, cut])).astype(BF16)
    for k in range(out_ref.shape[0]):
        out_ref[k] = r


def residual_second(
    y_ref, rinv_ref, innov_ref, inc_ref, old_ref, norm_ref, out_ref
):
    width = y_ref.shape[-1]
    cut = lanes(rank() * width, width)
    y = jnp.sum(y_ref[...].astype(F32), axis=0)
    r = (rinv_ref[:, :, cut] * (y - innov_ref[:, :, cut])).astype(BF16)
    blocks = [r[t, :, q * B : (q + 1) * B] for t in range(r.shape[0]) for q in range(width // B)]
    for k in range(out_ref.shape[0]):
        for q, block in enumerate(blocks):
            out_ref[k, q * r.shape[1] : (q + 1) * r.shape[1]] = block
    change = (old_ref[0].astype(F32) - r.astype(F32)) * (inc_ref[...] - y)
    change = jnp.sum(change.reshape(-1, 8, width), axis=0)
    norm = norm_ref[...].reshape(-1, 8, B).sum(axis=0)
    lane = lax.broadcasted_iota(jnp.int32, (16, B), 1)
    code = jnp.zeros((16, B), F32)
    for base, total in ((0, jnp.sum(norm)), (3, jnp.sum(change))):
        rest = jnp.full((16, B), total, F32)
        for k in range(3):
            piece = rest.astype(BF16).astype(F32)
            code = jnp.where(lane == base + k, piece, code)
            rest = rest - piece
    code = code.astype(BF16)
    for k in range(out_ref.shape[0]):
        out_ref[k, out_ref.shape[1] - 16 :] = code


def final_kernel(
    sums_ref, alpha_ref, chi_ref, sig_ref, acc1, acc2, prev1, next1, prev2, next2, res1, res2,
    an_ref, cn_ref, ga_ref, gc_ref,
):
    d = pl.program_id(0)
    members, total, width = an_ref.shape
    streams = len(acc1)
    levels = total // streams
    rows = width // B
    share = chi_ref.shape[0]
    cut = lanes(d * width, width)
    totals = sum(jnp.sum(s[...], axis=0, keepdims=True) for s in sums_ref)
    lane = lax.broadcasted_iota(jnp.int32, totals.shape, 1)
    norm = jnp.sum(jnp.where(lane < 3, totals, 0.0), axis=1, keepdims=True)
    prod = jnp.sum(jnp.where(lane < 6, totals, 0.0), axis=1, keepdims=True)
    step = norm / prod

    def rows_out(extra1, extra2):
        for h in range(streams):
            lv = slice(h * levels, (h + 1) * levels)
            for r in range(rows):
                sl = slice(r * B, (r + 1) * B)
                a1 = acc1[h][W + d * rows + r]
                a2 = acc2[h][W + d * rows + r]
                if extra1 is not None:
                    a1 = a1 + extra1(h, r).astype(F32)
                    a2 = a2 + extra2(h, r).astype(F32)
                a1 = a1.reshape(members, levels, B)
                a2 = a2.reshape(members, levels, B)
                a0 = alpha_ref[:, lv, lanes((d * rows + r) * B, B)]
                g = a0 + a1
                q = g + (a1 - a2)
                an_ref[:, lv, sl] = a0 - step[None] * g
                ga_ref[:, lv, sl] = g - step[None] * q

    last = pl.num_programs(0) - 1

    @pl.when(d == 0)
    def _():
        rows_out(lambda h, r: prev1[h][W + r], lambda h, r: prev2[h][r])

    @pl.when(d == last)
    def _():
        rows_out(lambda h, r: next1[h][r], lambda h, r: next2[h][r])

    @pl.when(jnp.logical_and(d > 0, d < last))
    def _():
        rows_out(None, None)

    def own_sum(res):
        parts = []
        for h in range(streams):
            s = jnp.concatenate(
                [
                    res_block(res[h], d, 0, r, rows, levels) + res_block(res[h], d, 1, r, rows, levels)
                    for r in range(rows)
                ],
                axis=1,
            )
            parts.append(gathered(masked(s, rank(), share, h * levels), share))
        return functools.reduce(jnp.add, parts)

    s1 = own_sum(res1)
    s2 = own_sum(res2)
    chi = chi_ref[:, cut]
    sg = sig_ref[:, cut]
    g = chi + sg * s1
    q = g + (sg * s1 - sg * s2)
    cn_ref[...] = chi - step * g
    gc_ref[...] = g - step * q


def body(anomalies, alpha0, chi0, sigma, innov, rinv, taper_cols, taper_coef):
    members, all_levels, columns = alpha0.shape
    slot_count = anomalies.shape[1]
    nblocks, slots = taper_cols.shape
    share = chi0.shape[0]
    groups = lax.axis_size("mem")
    tiles = lax.axis_size("tile")
    width = columns // groups
    levels = all_levels
    ml = members * levels
    padded = nblocks + 2 * W
    cols = taper_cols.T

    vm = pl.BlockSpec(memory_space=pltpu.VMEM)
    sm = pl.BlockSpec(memory_space=pltpu.SMEM)

    anywhere = pl.BlockSpec(memory_space=pltpu.HBM)
    part = functools.partial
    sds = jax.ShapeDtypeStruct
    pieces = sds((groups, slot_count, levels, width), BF16)
    inc_out = sds((slot_count, levels, width), F32)
    norm_out = sds((levels, B), F32)
    xs_out = sds((padded, ml, B), BF16)
    acc_out = sds((padded, ml, B), F32)
    work = 2 * ml * slots * B * B

    def call(kernel, name, scalars, operands, outs, scratch=(), limit=8, alias={}, hbm=0, rows=1):
        return pl.pallas_call(
            kernel,
            in_specs=[sm] * len(scalars) + [anywhere] * hbm + [vm] * (len(operands) - hbm),
            out_specs=[vm] * len(outs),
            out_shape=[pltpu.VMEM(o.shape, o.dtype) for o in outs],
            scratch_shapes=list(scratch),
            input_output_aliases={len(scalars) + k: v for k, v in alias.items()},
            compiler_params=pltpu.CompilerParams(vmem_limit_bytes=limit * MIB),
            cost_estimate=pl.CostEstimate(
                flops=8 * rows * work, transcendentals=0, bytes_accessed=rows * 3 * MIB // 4
            ),
            name=name,
        )(
            *scalars,
            *[pltpu.with_memory_space_constraint(o, pltpu.HBM) for o in operands[:hbm]],
            *[resident(o) for o in operands[hbm:]],
        )

    def exchanged(x):
        return lax.all_to_all(x, "mem", 0, 0)

    rim = sds((members, levels, W * B), BF16)
    high, low = call(
        edge_kernel, "edges", [], [alpha0], [rim, rim],
        [pltpu.VMEM((2, members, levels, W * B), F32), pltpu.SemaphoreType.DMA((2,))], hbm=1, rows=96,
    )
    low = shifted(low, "tile", 1)
    high = shifted(high, "tile", -1)
    alpha, xs1, part1, acc1, acc2 = call(
        first_inner, "first_inner", [cols], [alpha0, taper_coef, anomalies, chi0, sigma],
        [sds(alpha0.shape, F32), xs_out, pieces, acc_out, acc_out],
        [pltpu.SemaphoreType.DMA((groups,))], hbm=1, rows=24,
    )
    coef, anom = taper_coef, anomalies
    xs1, part1 = call(
        first_outer, "first_outer", [cols], [low, high, coef, anom, chi0, sigma, xs1, part1],
        [xs_out, pieces], alias={6: 0, 7: 1}, rows=8,
    )
    got1 = exchanged(part1)
    r1, inc1 = call(residual_first, "residual_first", [], [got1, rinv, innov], [pieces, inc_out])
    res1 = exchanged(r1)

    outer = 2 * W // (width // B)
    edge = sds((2 * W, ml, B), BF16)
    acc1, low1, high1 = call(
        part(adjoint_edges, outer), "adjoint_edges", [cols], [res1, anom, coef, acc1],
        [acc_out, edge, edge], alias={3: 0}, rows=16,
    )
    prev1 = shifted(high1, "tile", 1)
    next1 = shifted(low1, "tile", -1)
    acc1, xs2, part2, norm = call(
        part(second_inner, outer), "second_inner", [cols],
        [res1, anom, coef, alpha, chi0, sigma, acc1], [acc_out, xs_out, pieces, norm_out],
        alias={6: 0}, rows=32,
    )
    xs2, part2, norm = call(
        part(second_outer, outer), "second_outer", [cols],
        [res1, anom, coef, alpha, chi0, sigma, acc1, prev1, next1, xs2, part2, norm],
        [xs_out, pieces, norm_out], alias={9: 0, 10: 1, 11: 2}, rows=16,
    )
    got2 = exchanged(part2)
    (r2,) = call(
        residual_second, "residual_second", [], [got2, rinv, innov, inc1, r1, norm],
        [sds((groups, slot_count * levels * width // B + 16, B), BF16)],
    )
    res2 = exchanged(r2)
    edge = sds((W, ml, B), BF16)
    acc2, low2, high2, sums = call(
        adjoint_all, "adjoint_all", [cols], [res2, anom, coef, acc2],
        [acc_out, edge, edge, sds((tiles, B), F32)], alias={3: 0}, rows=32,
    )
    prev2 = shifted(high2, "tile", 1)
    next2 = shifted(low2, "tile", -1)
    sums = lax.all_to_all(sums, "tile", 0, 0, tiled=True)
    operands = [
        [sums], alpha, chi0, sigma, [acc1], [acc2], [prev1], [next1], [prev2], [next2], [res1], [res2]
    ]
    flat, tree = jax.tree.flatten(operands)
    count = len(flat)

    def final(*refs):
        final_kernel(*jax.tree.unflatten(tree, refs[:count]), *refs[count:])

    alpha_spec = pl.BlockSpec((members, all_levels, width), lambda d: (0, 0, d))
    chi_spec = pl.BlockSpec((share, width), lambda d: (0, d))
    out = pl.pallas_call(
        final,
        grid=(groups,),
        in_specs=[vm] * count,
        out_specs=[alpha_spec, chi_spec, alpha_spec, chi_spec],
        out_shape=[
            jax.ShapeDtypeStruct(alpha0.shape, F32),
            jax.ShapeDtypeStruct(chi0.shape, F32),
            jax.ShapeDtypeStruct(alpha0.shape, F32),
            jax.ShapeDtypeStruct(chi0.shape, F32),
        ],
        compiler_params=pltpu.CompilerParams(
            dimension_semantics=("arbitrary",), vmem_limit_bytes=8 * MIB
        ),
        name="final",
    )(*[resident(o) for o in flat])
    return tuple(out)


def solution(mesh):
    placed = (
        P("mem", None, None, "tile"),
        P("mem", None, "tile"),
        P("mem", "tile"),
        P("mem", "tile"),
        P(None, None, "tile"),
        P(None, None, "tile"),
        P("tile", None),
        P("tile", None, None, None),
    )
    return jax.shard_map(
        body,
        mesh=mesh,
        in_specs=placed,
        out_specs=(
            P("mem", None, "tile"),
            P("mem", "tile"),
            P("mem", None, "tile"),
            P("mem", "tile"),
        ),
        check_vma=False,
    )
```

```python
import functools
import jax
import jax.numpy as jnp
from jax import lax
from jax.experimental import pallas as pl
from jax.experimental.pallas import tpu as pltpu
from jax.sharding import PartitionSpec as P

W = 4
B = 128
F32 = jnp.float32
BF16 = jnp.bfloat16
MIB = 2**20


def shifted(array, axis, by):
    size = lax.axis_size(axis)
    return lax.ppermute(array, axis, [(i, (i + by) % size) for i in range(size)])


def resident(array):
    return pltpu.with_memory_space_constraint(array, pltpu.VMEM)


def column(cols, i, s):
    nblocks = cols.shape[1]
    total = nblocks * lax.axis_size("tile")
    c = cols[s, i] - lax.axis_index("tile").astype(jnp.int32) * nblocks + W
    c = jnp.where(c < 0, c + total, c)
    return jnp.where(c >= total, c - total, c)


def rank():
    return lax.axis_index("mem").astype(jnp.int32)


def masked(full, me, share, first):
    level = first + lax.broadcasted_iota(jnp.int32, full.shape, 0)
    mine = jnp.logical_and(level >= me * share, level < (me + 1) * share)
    return jnp.where(mine, full, 0.0)


def spread(own, me, levels, first):
    share = own.shape[0]
    return masked(jnp.concatenate([own] * (levels // share), axis=0), me, share, first)


def gathered(full, share):
    parts = [full[g * share : (g + 1) * share] for g in range(full.shape[0] // share)]
    return functools.reduce(jnp.add, parts)


def lanes(start, size):
    return pl.ds(pl.multiple_of(start, B), size)


def localize_group(d, levels, first, cols, xs, coef_ref, anom_ref, out_ref, static):
    groups = out_ref.shape[0]
    nblocks, slots = coef_ref.shape[:2]
    members, slot_count = anom_ref.shape[:2]
    rows = nblocks // groups
    lv = slice(first, first + levels)
    for r in range(rows):
        i = d * rows + r
        sl = slice(r * B, (r + 1) * B)
        lhs = jnp.concatenate([xs[column(cols, i, s)] for s in range(slots)], axis=1)
        rhs = jnp.concatenate([coef_ref[i, s] for s in range(slots)], axis=1)
        loc = lax.dot_general(
            lhs, rhs, (((1,), (1,)), ((), ())), preferred_element_type=F32
        ).reshape(members, levels, B)
        for t in range(slot_count):
            a = anom_ref[:, t, lv, lanes(i * B, B)].astype(F32)
            inc = jnp.sum(a * loc, axis=0) + static[:, sl]
            out_ref[d, t, :, sl] = inc.astype(BF16)


def first_static(d, width, levels, chi_ref, sig_ref):
    cut = lanes(d * width, width)
    return spread(sig_ref[:, cut] * chi_ref[:, cut], rank(), levels, 0)


def second_static(d, width, levels, chi_ref, sig_ref, res_ref, norm_ref):
    cut = lanes(d * width, width)
    rsum = res_ref[d, 0].astype(F32) + res_ref[d, 1].astype(F32)
    sig = spread(sig_ref[:, cut], rank(), levels, 0)
    chi = spread(chi_ref[:, cut], rank(), levels, 0)
    sr = sig * rsum
    gc = chi + sr
    sq = gc * gc
    for r in range(width // B):
        norm_ref[...] += sq[:, r * B : (r + 1) * B]
    return -(sig * sr)


def edge_kernel(alpha_hbm, low_ref, high_ref, buf, sem):
    columns = alpha_hbm.shape[-1]
    width = low_ref.shape[-1]
    copies = [
        pltpu.make_async_copy(alpha_hbm.at[:, :, pl.ds(start, width)], buf.at[k], sem.at[k])
        for k, start in enumerate((0, columns - width))
    ]
    for c in copies:
        c.start()
    for c, out in zip(copies, (low_ref, high_ref)):
        c.wait()
        out[...] = buf[0 if out is low_ref else 1].astype(BF16)


def first_inner(
    cols, alpha_hbm, coef_ref, anom_ref, chi_ref, sig_ref, alpha_ref, xs, out_ref, zero_a, zero_b, sem
):
    members, levels, columns = alpha_ref.shape
    groups = out_ref.shape[0]
    width = columns // groups
    rows = width // B
    ml = members * levels

    def copy(d):
        part = (slice(None), slice(None), pl.ds(d * width, width))
        return pltpu.make_async_copy(alpha_hbm.at[part], alpha_ref.at[part], sem.at[d])

    for d in range(groups):
        copy(d).start()

    def clear(b, carry):
        zero_a[b] = jnp.zeros(zero_a.shape[1:], F32)
        zero_b[b] = jnp.zeros(zero_b.shape[1:], F32)
        return carry

    lax.fori_loop(0, zero_a.shape[0], clear, 0)

    def load(d):
        copy(d).wait()
        for r in range(rows):
            b = d * rows + r
            xs[W + b] = alpha_ref[:, :, b * B : (b + 1) * B].astype(BF16).reshape(ml, B)

    load(0)
    load(1)
    for d in range(1, groups - 1):
        load(d + 1)
        static = first_static(d, width, levels, chi_ref, sig_ref)
        localize_group(d, levels, 0, cols, xs, coef_ref, anom_ref, out_ref, static)


def first_outer(
    cols, low_ref, high_ref, coef_ref, anom_ref, chi_ref, sig_ref, xs_in, part_ref, xs, out_ref
):
    members, _, levels, columns = anom_ref.shape
    groups = out_ref.shape[0]
    width = columns // groups
    ml = members * levels
    n = columns // B
    for b in range(W):
        xs[b] = low_ref[:, :, b * B : (b + 1) * B].reshape(ml, B)
        xs[W + n + b] = high_ref[:, :, b * B : (b + 1) * B].reshape(ml, B)

    def step(k, carry):
        d = k * (groups - 1)
        static = first_static(d, width, levels, chi_ref, sig_ref)
        localize_group(d, levels, 0, cols, xs, coef_ref, anom_ref, out_ref, static)
        return carry

    lax.fori_loop(0, 2, step, 0, unroll=2)


def res_block(res_ref, d, t, r, rows, levels):
    if len(res_ref.shape) == 4:
        return res_ref[d, t, :, r * B : (r + 1) * B].astype(F32)
    base = (t * rows + r) * levels
    return res_ref[d, base : base + levels].astype(F32)


def adjoint_group(d, cols, res_ref, anom_ref, coef_ref, acc_ref):
    groups = res_ref.shape[0]
    nblocks, slots = coef_ref.shape[:2]
    members, slot_count, levels = anom_ref.shape[:3]
    rows = nblocks // groups
    for r in range(rows):
        i = d * rows + r
        sl = slice(r * B, (r + 1) * B)
        w = functools.reduce(
            jnp.add,
            [
                anom_ref[:, t, :, lanes(i * B, B)].astype(F32)
                * res_block(res_ref, d, t, r, rows, levels)[None]
                for t in range(slot_count)
            ],
        )
        w = w.astype(BF16).reshape(members * levels, B)
        for s in range(slots):
            acc_ref[column(cols, i, s)] += jnp.dot(w, coef_ref[i, s], preferred_element_type=F32)


def adjoint_edges(outer, cols, res_ref, anom_ref, coef_ref, acc_in, acc_ref, low_ref, high_ref):
    groups = res_ref.shape[0]
    padded = acc_ref.shape[0]

    def step(k, carry):
        d = jnp.where(k < outer, k, groups - 2 * outer + k)
        adjoint_group(d, cols, res_ref, anom_ref, coef_ref, acc_ref)
        return carry

    lax.fori_loop(0, 2 * outer, step, 0, unroll=2)
    halo = low_ref.shape[0]
    for b in range(halo):
        low_ref[b] = acc_ref[b].astype(BF16)
        high_ref[b] = acc_ref[padded - halo + b].astype(BF16)


def adjoint_all(cols, res_ref, anom_ref, coef_ref, acc_in, acc_ref, low_ref, high_ref, sum_ref):
    groups = res_ref.shape[0]
    code = functools.reduce(jnp.add, [res_ref[d, res_ref.shape[1] - 16 :].astype(F32) for d in range(groups)])
    sum_ref[...] = jnp.broadcast_to(code[:1], sum_ref.shape)
    outer = res_ref.shape[0] // 2
    adjoint_edges(outer, cols, res_ref, anom_ref, coef_ref, acc_in, acc_ref, low_ref, high_ref)


def adjoint_rest(outer, cols, res_ref, anom_ref, coef_ref, acc_in, acc_ref):
    def step(d, carry):
        adjoint_group(d, cols, res_ref, anom_ref, coef_ref, acc_ref)
        return carry

    lax.fori_loop(outer, res_ref.shape[0] - outer, step, 0, unroll=2)


def second_block(b, adj, alpha_ref, xs, norm_ref, own):
    members, levels = alpha_ref.shape[:2]
    xs[b] = (-adj).astype(BF16)
    if own:
        g = alpha_ref[:, :, lanes((b - W) * B, B)] + adj.reshape(members, levels, B)
        norm_ref[...] += jnp.sum(g * g, axis=0)


def second_inner(
    outer, cols, res_ref, anom_ref, coef_ref, alpha_ref, chi_ref, sig_ref, acc_in,
    acc_ref, xs, out_ref, norm_ref,
):
    adjoint_rest(outer, cols, res_ref, anom_ref, coef_ref, acc_in, acc_ref)
    levels = alpha_ref.shape[1]
    groups = out_ref.shape[0]
    padded = acc_ref.shape[0]
    width = out_ref.shape[-1]
    norm_ref[...] = jnp.zeros_like(norm_ref)

    def block(b, carry):
        second_block(b, acc_ref[b], alpha_ref, xs, norm_ref, True)
        return carry

    lax.fori_loop(2 * W, padded - 2 * W, block, 0, unroll=2)

    def step(d, carry):
        static = second_static(d, width, levels, chi_ref, sig_ref, res_ref, norm_ref)
        localize_group(d, levels, 0, cols, xs, coef_ref, anom_ref, out_ref, static)
        return carry

    lax.fori_loop(outer, groups - outer, step, 0, unroll=2)


def second_outer(
    outer, cols, res_ref, anom_ref, coef_ref, alpha_ref, chi_ref, sig_ref, acc_ref, prev_ref,
    next_ref, xs_in, part_in, norm_in, xs, out_ref, norm_ref,
):
    levels = alpha_ref.shape[1]
    groups = out_ref.shape[0]
    width = out_ref.shape[-1]
    n = acc_ref.shape[0] - 2 * W
    for b in range(2 * W):
        second_block(b, acc_ref[b] + prev_ref[b].astype(F32), alpha_ref, xs, norm_ref, b >= W)
        second_block(n + b, acc_ref[n + b] + next_ref[b].astype(F32), alpha_ref, xs, norm_ref, b < W)

    def step(k, carry):
        d = jnp.where(k < outer, k, groups - 2 * outer + k)
        static = second_static(d, width, levels, chi_ref, sig_ref, res_ref, norm_ref)
        localize_group(d, levels, 0, cols, xs, coef_ref, anom_ref, out_ref, static)
        return carry

    lax.fori_loop(0, 2 * outer, step, 0, unroll=2)


def residual_first(y_ref, rinv_ref, innov_ref, out_ref, inc_ref):
    width = y_ref.shape[-1]
    cut = lanes(rank() * width, width)
    y = jnp.sum(y_ref[...].astype(F32), axis=0)
    inc_ref[...] = y
    r = (rinv_ref[:, :, cut] * (y - innov_ref[:, :, cut])).astype(BF16)
    for k in range(out_ref.shape[0]):
        out_ref[k] = r


def residual_second(
    y_ref, rinv_ref, innov_ref, inc_ref, old_ref, norm_ref, out_ref
):
    width = y_ref.shape[-1]
    cut = lanes(rank() * width, width)
    y = jnp.sum(y_ref[...].astype(F32), axis=0)
    r = (rinv_ref[:, :, cut] * (y - innov_ref[:, :, cut])).astype(BF16)
    blocks = [r[t, :, q * B : (q + 1) * B] for t in range(r.shape[0]) for q in range(width // B)]
    for k in range(out_ref.shape[0]):
        for q, block in enumerate(blocks):
            out_ref[k, q * r.shape[1] : (q + 1) * r.shape[1]] = block
    change = (old_ref[0].astype(F32) - r.astype(F32)) * (inc_ref[...] - y)
    change = jnp.sum(change.reshape(-1, 8, width), axis=0)
    norm = norm_ref[...].reshape(-1, 8, B).sum(axis=0)
    lane = lax.broadcasted_iota(jnp.int32, (16, B), 1)
    code = jnp.zeros((16, B), F32)
    for base, total in ((0, jnp.sum(norm)), (3, jnp.sum(change))):
        rest = jnp.full((16, B), total, F32)
        for k in range(3):
            piece = rest.astype(BF16).astype(F32)
            code = jnp.where(lane == base + k, piece, code)
            rest = rest - piece
    code = code.astype(BF16)
    for k in range(out_ref.shape[0]):
        out_ref[k, out_ref.shape[1] - 16 :] = code


def final_kernel(
    sums_ref, alpha_ref, chi_ref, sig_ref, acc1, acc2, prev1, next1, prev2, next2, res1, res2,
    an_ref, cn_ref, ga_ref, gc_ref,
):
    d = pl.program_id(0)
    members, total, width = an_ref.shape
    streams = len(acc1)
    levels = total // streams
    rows = width // B
    share = chi_ref.shape[0]
    cut = lanes(d * width, width)
    totals = sum(jnp.sum(s[...], axis=0, keepdims=True) for s in sums_ref)
    lane = lax.broadcasted_iota(jnp.int32, totals.shape, 1)
    norm = jnp.sum(jnp.where(lane < 3, totals, 0.0), axis=1, keepdims=True)
    prod = jnp.sum(jnp.where(lane < 6, totals, 0.0), axis=1, keepdims=True)
    step = norm / prod

    def rows_out(extra1, extra2):
        for h in range(streams):
            lv = slice(h * levels, (h + 1) * levels)
            for r in range(rows):
                sl = slice(r * B, (r + 1) * B)
                a1 = acc1[h][W + d * rows + r]
                a2 = acc2[h][W + d * rows + r]
                if extra1 is not None:
                    a1 = a1 + extra1(h, r).astype(F32)
                    a2 = a2 + extra2(h, r).astype(F32)
                a1 = a1.reshape(members, levels, B)
                a2 = a2.reshape(members, levels, B)
                a0 = alpha_ref[:, lv, lanes((d * rows + r) * B, B)]
                g = a0 + a1
                q = g + (a1 - a2)
                an_ref[:, lv, sl] = a0 - step[None] * g
                ga_ref[:, lv, sl] = g - step[None] * q

    last = pl.num_programs(0) - 1

    @pl.when(d == 0)
    def _():
        rows_out(lambda h, r: prev1[h][W + r], lambda h, r: prev2[h][r])

    @pl.when(d == last)
    def _():
        rows_out(lambda h, r: next1[h][r], lambda h, r: next2[h][r])

    @pl.when(jnp.logical_and(d > 0, d < last))
    def _():
        rows_out(None, None)

    def own_sum(res):
        parts = []
        for h in range(streams):
            s = jnp.concatenate(
                [
                    res_block(res[h], d, 0, r, rows, levels) + res_block(res[h], d, 1, r, rows, levels)
                    for r in range(rows)
                ],
                axis=1,
            )
            parts.append(gathered(masked(s, rank(), share, h * levels), share))
        return functools.reduce(jnp.add, parts)

    s1 = own_sum(res1)
    s2 = own_sum(res2)
    chi = chi_ref[:, cut]
    sg = sig_ref[:, cut]
    g = chi + sg * s1
    q = g + (sg * s1 - sg * s2)
    cn_ref[...] = chi - step * g
    gc_ref[...] = g - step * q


def body(anomalies, alpha0, chi0, sigma, innov, rinv, taper_cols, taper_coef):
    members, all_levels, columns = alpha0.shape
    slot_count = anomalies.shape[1]
    nblocks, slots = taper_cols.shape
    share = chi0.shape[0]
    groups = lax.axis_size("mem")
    tiles = lax.axis_size("tile")
    width = columns // groups
    levels = all_levels
    ml = members * levels
    padded = nblocks + 2 * W
    cols = taper_cols.T

    vm = pl.BlockSpec(memory_space=pltpu.VMEM)
    sm = pl.BlockSpec(memory_space=pltpu.SMEM)

    anywhere = pl.BlockSpec(memory_space=pltpu.HBM)
    part = functools.partial
    sds = jax.ShapeDtypeStruct
    pieces = sds((groups, slot_count, levels, width), BF16)
    inc_out = sds((slot_count, levels, width), F32)
    norm_out = sds((levels, B), F32)
    xs_out = sds((padded, ml, B), BF16)
    acc_out = sds((padded, ml, B), F32)
    work = 2 * ml * slots * B * B

    def call(kernel, name, scalars, operands, outs, scratch=(), limit=8, alias={}, hbm=0, rows=1):
        return pl.pallas_call(
            kernel,
            in_specs=[sm] * len(scalars) + [anywhere] * hbm + [vm] * (len(operands) - hbm),
            out_specs=[vm] * len(outs),
            out_shape=[pltpu.VMEM(o.shape, o.dtype) for o in outs],
            scratch_shapes=list(scratch),
            input_output_aliases={len(scalars) + k: v for k, v in alias.items()},
            compiler_params=pltpu.CompilerParams(vmem_limit_bytes=limit * MIB),
            cost_estimate=pl.CostEstimate(
                flops=8 * rows * work, transcendentals=0, bytes_accessed=rows * 3 * MIB // 4
            ),
            name=name,
        )(
            *scalars,
            *[pltpu.with_memory_space_constraint(o, pltpu.HBM) for o in operands[:hbm]],
            *[resident(o) for o in operands[hbm:]],
        )

    def exchanged(x):
        return lax.all_to_all(x, "mem", 0, 0)

    rim = sds((members, levels, W * B), BF16)
    high, low = call(
        edge_kernel, "edges", [], [alpha0], [rim, rim],
        [pltpu.VMEM((2, members, levels, W * B), F32), pltpu.SemaphoreType.DMA((2,))], hbm=1, rows=96,
    )
    low = shifted(low, "tile", 1)
    high = shifted(high, "tile", -1)
    alpha, xs1, part1, acc1, acc2 = call(
        first_inner, "first_inner", [cols], [alpha0, taper_coef, anomalies, chi0, sigma],
        [sds(alpha0.shape, F32), xs_out, pieces, acc_out, acc_out],
        [pltpu.SemaphoreType.DMA((groups,))], hbm=1, rows=24,
    )
    coef, anom = taper_coef, anomalies
    xs1, part1 = call(
        first_outer, "first_outer", [cols], [low, high, coef, anom, chi0, sigma, xs1, part1],
        [xs_out, pieces], alias={6: 0, 7: 1}, rows=8,
    )
    got1 = exchanged(part1)
    r1, inc1 = call(residual_first, "residual_first", [], [got1, rinv, innov], [pieces, inc_out])
    res1 = exchanged(r1)

    outer = 2 * W // (width // B)
    edge = sds((2 * W, ml, B), BF16)
    acc1, low1, high1 = call(
        part(adjoint_edges, outer), "adjoint_edges", [cols], [res1, anom, coef, acc1],
        [acc_out, edge, edge], alias={3: 0}, rows=16,
    )
    prev1 = shifted(high1, "tile", 1)
    next1 = shifted(low1, "tile", -1)
    acc1, xs2, part2, norm = call(
        part(second_inner, outer), "second_inner", [cols],
        [res1, anom, coef, alpha, chi0, sigma, acc1], [acc_out, xs_out, pieces, norm_out],
        alias={6: 0}, rows=32,
    )
    xs2, part2, norm = call(
        part(second_outer, outer), "second_outer", [cols],
        [res1, anom, coef, alpha, chi0, sigma, acc1, prev1, next1, xs2, part2, norm],
        [xs_out, pieces, norm_out], alias={9: 0, 10: 1, 11: 2}, rows=16,
    )
    got2 = exchanged(part2)
    (r2,) = call(
        residual_second, "residual_second", [], [got2, rinv, innov, inc1, r1, norm],
        [sds((groups, slot_count * levels * width // B + 16, B), BF16)],
    )
    res2 = exchanged(r2)
    edge = sds((W, ml, B), BF16)
    acc2, low2, high2, sums = call(
        adjoint_all, "adjoint_all", [cols], [res2, anom, coef, acc2],
        [acc_out, edge, edge, sds((tiles, B), F32)], alias={3: 0}, rows=32,
    )
    prev2 = shifted(high2, "tile", 1)
    next2 = shifted(low2, "tile", -1)
    sums = lax.all_to_all(sums, "tile", 0, 0, tiled=True)
    operands = [
        [sums], alpha, chi0, sigma, [acc1], [acc2], [prev1], [next1], [prev2], [next2], [res1], [res2]
    ]
    flat, tree = jax.tree.flatten(operands)
    count = len(flat)

    def final(*refs):
        final_kernel(*jax.tree.unflatten(tree, refs[:count]), *refs[count:])

    alpha_spec = pl.BlockSpec((members, all_levels, width), lambda d: (0, 0, d))
    chi_spec = pl.BlockSpec((share, width), lambda d: (0, d))
    out = pl.pallas_call(
        final,
        grid=(groups,),
        in_specs=[vm] * count,
        out_specs=[alpha_spec, chi_spec, alpha_spec, chi_spec],
        out_shape=[
            jax.ShapeDtypeStruct(alpha0.shape, F32),
            jax.ShapeDtypeStruct(chi0.shape, F32),
            jax.ShapeDtypeStruct(alpha0.shape, F32),
            jax.ShapeDtypeStruct(chi0.shape, F32),
        ],
        compiler_params=pltpu.CompilerParams(
            dimension_semantics=("arbitrary",), vmem_limit_bytes=8 * MIB
        ),
        name="final",
    )(*[resident(o) for o in flat])
    return tuple(out)


def solution(mesh):
    placed = (
        P("mem", None, None, "tile"),
        P("mem", None, "tile"),
        P("mem", "tile"),
        P("mem", "tile"),
        P(None, None, "tile"),
        P(None, None, "tile"),
        P("tile", None),
        P("tile", None, None, None),
    )
    return jax.shard_map(
        body,
        mesh=mesh,
        in_specs=placed,
        out_specs=(
            P("mem", None, "tile"),
            P("mem", "tile"),
            P("mem", None, "tile"),
            P("mem", "tile"),
        ),
        check_vma=False,
    )
```
